128 devices in a mesh: leaf: 4 (over x), front: 32 (over z, y, core).
Axes of the slice: x: 4, y: 4, z: 4, core: 2. Of those that a mesh axis runs over, the one named last changes fastest.
Arguments:
- probe_seeds: int32 [32], replicated, may hold values from 0 to 32748
- leaf_inverse: bfloat16 [4, 4096, 4096], P('leaf', 'front'), as said below
- leaf_update: bfloat16 [4, 4096, 16384], P('leaf', 'front'), may hold values from -0.046875 to 0.046875
- internal_inverse: bfloat16 [4, 4096, 4096], P('leaf', 'front'), as said below
- internal_update: bfloat16 [4, 4096, 16384], P('leaf', 'front'), may hold values from -0.046875 to 0.046875
- child_map: int32 [4, 2, 256], P('leaf'), may hold values from 0 to 320, as said below
Outputs:
- leaf_solution: float32 [4, 32, 4096], P('leaf', None, 'front')
- internal_solution: float32 [4, 32, 4096], P('leaf', None, 'front')
The draws below stay inside these ranges and needn't reach their ends.
Inputs may be any that keep to these rules, and one draw needn't show every extreme that they name: `child_map`: in each row of a slot and child the entries other than 320 are distinct; the last row is not read. `leaf_inverse`: each supernode's matrix is lower triangular with a positive diagonal. `internal_inverse`: each slot's matrix is lower triangular with a positive diagonal.
All inputs are finite; a program needn't handle non-finite values.
Results may differ from the reference program's by a relative error of at most 0.0065.
Values may be sent and summed in bfloat16 or wider, within the bound.
A program may use at most 64 MiB of HBM per device.

```python
import math
import jax
import jax.numpy as jnp
import numpy as np
from jax import lax

BLOCK = 64
PROBES = 32
LEAVES = 4
NB = 64
UPD = 256
COLS = 4096


def lower_factor(key):
    diag_key, below_key = jax.random.split(key)
    diagonal = jnp.exp(jax.random.uniform(diag_key, (LEAVES, COLS), jnp.float32, math.log(0.5), math.log(2.0)))
    below = jax.random.normal(below_key, (LEAVES, COLS, COLS), jnp.float32)
    positions = jnp.arange(COLS, dtype=jnp.int32)
    strictly = positions[:, None] > positions[None, :]
    equal_pos = positions[:, None] == positions[None, :]
    scaled = jnp.where(strictly[None, :, :], below * (1.0 / math.sqrt(COLS)), 0.0)
    full_matrix = scaled + jnp.where(equal_pos[None, :, :], diagonal[:, :, None], 0.0)
    return full_matrix.astype(jnp.bfloat16)


def draw_leaf_inverse(key, part):
    return lower_factor(jax.random.fold_in(key, 5))


def draw_internal_inverse(key, part):
    return lower_factor(jax.random.fold_in(key, 11))


def draw_child_map(key, part):
    score_key, blank_key = jax.random.split(jax.random.fold_in(key, 17))
    front_blocks = NB + UPD
    scores = jax.random.randint(score_key, (LEAVES, 2, front_blocks), 0, 1 << 20, dtype=jnp.int32)
    scores = scores * front_blocks + jnp.arange(front_blocks, dtype=jnp.int32)[None, None, :]
    ordering = jnp.argsort(scores, axis=-1, stable=True)[:, :, :UPD].astype(jnp.int32)
    blanks = jax.random.randint(blank_key, (LEAVES, 2, UPD), 0, 4, dtype=jnp.int32) == 0
    return jnp.where(blanks, front_blocks, ordering).astype(jnp.int32)


def touch_ends(entries, rng, smallest, top_value):
    index_at = [jax.random.randint(jax.random.fold_in(rng, axis), (), 0, length) for axis, length in enumerate(entries.shape)]
    main_axis = entries.shape.index(max(entries.shape))
    next_to = index_at[:main_axis] + [(index_at[main_axis] + 1) % entries.shape[main_axis]] + index_at[main_axis + 1:]
    return entries.at[tuple(index_at)].set(smallest).at[tuple(next_to)].set(top_value)


def block_scale(stream_key, shape, shards, least, high):
    loudness, own = 1.0, jax.random.fold_in(stream_key, 6)
    for dim, blocks in shards:
        steps = jnp.exp(jax.random.uniform(jax.random.fold_in(own, dim), (blocks,), jnp.float32, least / len(shards), high / len(shards)))
        loudness = loudness * jnp.repeat(steps, shape[dim] // blocks).reshape([-1 if axis == dim else 1 for axis in range(len(shape))])
    return loudness


def bell_draw(rng, shape, spread, reach, cuts=(), held_as=jnp.bfloat16):
    values = jax.random.normal(rng, shape, jnp.float32) * spread
    if len(cuts) > 0:
        values = block_scale(rng, shape, cuts, -0.22, 0.18) * values
    return jnp.clip(values, min=-reach, max=reach).astype(held_as)


def setup_inputs(seed: int = 0) -> dict:
    arg_keys = jax.random.split(jax.random.key(seed), 7)
    return {
        "probe_seeds": touch_ends(jax.random.randint(arg_keys[0], (PROBES,), 0, 32749), jax.random.fold_in(arg_keys[0], 1), 0, 32748).astype(jnp.int32),
        "leaf_inverse": draw_leaf_inverse(jax.random.fold_in(arg_keys[6], 71), 0),
        "leaf_update": bell_draw(arg_keys[2], (LEAVES, COLS, UPD * BLOCK), (4 * COLS) ** -0.5, 0.046875, ((0, 4), (1, 32))),
        "internal_inverse": draw_internal_inverse(jax.random.fold_in(arg_keys[6], 71), 0),
        "internal_update": bell_draw(arg_keys[4], (LEAVES, COLS, UPD * BLOCK), (4 * COLS) ** -0.5, 0.046875, ((0, 4), (1, 32))),
        "child_map": draw_child_map(jax.random.fold_in(arg_keys[6], 71), 0),
    }


HIGHEST = lax.Precision.HIGHEST


def probe_signs(seeds, node_id, columns):
    index = node_id * columns + jnp.arange(columns, dtype=jnp.int32)
    lower = index % 32749
    upper = index // 32749
    hashed = (lower * 30011 + upper * 7717 + seeds[:, None]) % 32749
    hashed = (hashed * hashed) % 32749
    hashed = (hashed * 21143 + lower) % 32749
    hashed = (hashed * hashed + upper) % 32749
    return (1 - 2 * ((hashed // 8) % 2)).astype(jnp.bfloat16)


def place_blocks(vectors, targets, front_blocks):
    onehot = (targets[:, :, None] == jnp.arange(front_blocks, dtype=jnp.int32)[None, None, :]).astype(jnp.float32)
    shaped = vectors.reshape(vectors.shape[0], vectors.shape[1], targets.shape[1], BLOCK)
    placed = jnp.einsum('npkb,nkt->nptb', shaped, onehot, precision=HIGHEST)
    return placed.reshape(vectors.shape[0], vectors.shape[1], front_blocks * BLOCK)


def pick_blocks(front_vector, targets, front_blocks):
    onehot = (targets[:, :, None] == jnp.arange(front_blocks, dtype=jnp.int32)[None, None, :]).astype(jnp.float32)
    shaped = front_vector.astype(jnp.float32).reshape(front_vector.shape[0], front_vector.shape[1], front_blocks, BLOCK)
    picked = jnp.einsum('nptb,nkt->npkb', shaped, onehot, precision=HIGHEST).astype(jnp.bfloat16)
    return picked.reshape(front_vector.shape[0], front_vector.shape[1], targets.shape[1] * BLOCK)


def apply_inverse(right_side, inverse):
    return jnp.einsum('npj,nij->npi', right_side.astype(jnp.float32), inverse.astype(jnp.float32))


def apply_transposed(right_side, inverse):
    return jnp.einsum('npi,nij->npj', right_side.astype(jnp.float32), inverse.astype(jnp.float32))


def push_update(solved, update):
    return jnp.einsum('npi,niu->npu', solved.astype(jnp.float32), update.astype(jnp.float32))


def pull_update(incoming, update):
    return jnp.einsum('npu,niu->npi', incoming.astype(jnp.float32), update.astype(jnp.float32))


def reference(probe_seeds, leaf_inverse, leaf_update, internal_inverse, internal_update, child_map):
    leaves = leaf_inverse.shape[0]
    columns = leaf_inverse.shape[1]
    col_blocks = columns // BLOCK
    upd_blocks = leaf_update.shape[2] // BLOCK
    front_blocks = col_blocks + upd_blocks
    probe_count = probe_seeds.shape[0]
    heights = leaves.bit_length() - 1
    node_ids = jnp.arange(leaves, dtype=jnp.int32)
    signer = jax.vmap(probe_signs, in_axes=(None, 0, None))
    leaf_signs = signer(probe_seeds, node_ids, columns)
    inner_signs = signer(probe_seeds, node_ids + leaves, columns)

    leaf_solved = apply_inverse(leaf_signs, leaf_inverse)
    leaf_sent = push_update(leaf_solved.astype(jnp.bfloat16), leaf_update)
    inner_solved = jnp.zeros((leaves, probe_count, columns), jnp.float32)
    inner_sent = jnp.zeros((leaves, probe_count, upd_blocks * BLOCK), jnp.float32)
    for height in range(1, heights + 1):
        half_span = 2 ** (height - 1)
        slot_ids = np.arange(half_span, leaves, 2 * half_span)
        rows = slot_ids - 1
        if height == 1:
            left_sent = leaf_sent[slot_ids - 1]
            right_sent = leaf_sent[slot_ids]
        else:
            distance = half_span // 2
            left_sent = inner_sent[slot_ids - distance]
            right_sent = inner_sent[slot_ids + distance]
        lists_now = child_map[rows]
        gathered = place_blocks(left_sent, lists_now[:, 0], front_blocks) + place_blocks(right_sent, lists_now[:, 1], front_blocks)
        residual = (inner_signs[slot_ids].astype(jnp.float32) - gathered[:, :, :columns]).astype(jnp.bfloat16)
        solved = apply_inverse(residual, internal_inverse[rows])
        sent = gathered[:, :, columns:] + push_update(solved.astype(jnp.bfloat16), internal_update[rows])
        inner_solved = inner_solved.at[slot_ids].set(solved)
        inner_sent = inner_sent.at[slot_ids].set(sent)

    inner_result = jnp.zeros((leaves, probe_count, columns), jnp.float32)
    inner_incoming = jnp.zeros((leaves, probe_count, upd_blocks * BLOCK), jnp.bfloat16)
    leaf_incoming = jnp.zeros((leaves, probe_count, upd_blocks * BLOCK), jnp.bfloat16)
    for height in range(heights, 0, -1):
        half_span = 2 ** (height - 1)
        slot_ids = np.arange(half_span, leaves, 2 * half_span)
        rows = slot_ids - 1
        incoming = inner_incoming[slot_ids]
        scaled = (inner_solved[slot_ids] - pull_update(incoming, internal_update[rows])).astype(jnp.bfloat16)
        solution = apply_transposed(scaled, internal_inverse[rows])
        inner_result = inner_result.at[rows].set(solution)
        front_vector = jnp.concatenate([solution.astype(jnp.bfloat16), incoming], axis=2)
        lists_now = child_map[rows]
        for_left = pick_blocks(front_vector, lists_now[:, 0], front_blocks)
        for_right = pick_blocks(front_vector, lists_now[:, 1], front_blocks)
        if height == 1:
            leaf_incoming = leaf_incoming.at[slot_ids - 1].set(for_left)
            leaf_incoming = leaf_incoming.at[slot_ids].set(for_right)
        else:
            distance = half_span // 2
            inner_incoming = inner_incoming.at[slot_ids - distance].set(for_left)
            inner_incoming = inner_incoming.at[slot_ids + distance].set(for_right)
    leaf_scaled = (leaf_solved - pull_update(leaf_incoming, leaf_update)).astype(jnp.bfloat16)
    leaf_result = apply_transposed(leaf_scaled, leaf_inverse)
    return leaf_result, inner_result
```

```python
import functools

import jax
import jax.numpy as jnp
from jax import lax
from jax.experimental import pallas as pl
from jax.experimental.pallas import tpu as pltpu
from jax.sharding import PartitionSpec as P

BLOCK = 64
MOD = 32749
MESH = pl.DeviceIdType.MESH
NT = (((1,), (1,)), ((), ()))


def mod_prime(x):
    q = (x.astype(jnp.float32) * (1.0 / MOD)).astype(jnp.int32)
    r = x - q * MOD
    r = jnp.where(r < 0, r + MOD, r)
    return jnp.where(r >= MOD, r - MOD, r)


def probe_signs(seeds, node_id, columns, start, shape):
    index = node_id * columns + start + lax.broadcasted_iota(jnp.int32, shape, 1)
    wrapped = index >= MOD
    lower = jnp.where(wrapped, index - MOD, index)
    upper = jnp.where(wrapped, 1, 0)
    hashed = mod_prime(lower * 30011 + upper * 7717 + seeds)
    hashed = mod_prime(hashed * hashed)
    hashed = mod_prime(hashed * 21143 + lower)
    hashed = mod_prime(hashed * hashed + upper)
    return (1 - 2 * ((hashed >> 3) & 1)).astype(jnp.float32)


def kernel(
    fronts,
    probes,
    columns,
    width,
    seeds_ref,
    maps_ref,
    leaf_inv_hbm,
    leaf_upd_hbm,
    inner_inv_hbm,
    inner_upd_hbm,
    leaf_out,
    inner_out,
    leaf_inv,
    leaf_upd,
    inner_inv,
    inner_upd,
    to_slot,
    to_root,
    slot_root,
    signs,
    all_maps,
    table_v,
    table_s,
    send_part,
    recv_part,
    own_chunk,
    recv_all,
    hop_send,
    hop_up,
    hop_root,
    hop_chunk,
    leaf_y,
    leaf_v,
    load_sem,
    table_sem,
    map_send,
    map_recv,
    part_send,
    part_recv,
    all_send,
    all_recv,
    hop_send_sem,
    hop_up_sem,
    hop_root_sem,
    hop_chunk_sem,
):
    x = lax.axis_index("leaf")
    m = lax.axis_index("front")
    leaves = 4
    f32, bf16 = jnp.float32, jnp.bfloat16
    is_slot = (x == 0) | (x == 2)
    is_root = x == 1

    loads = [
        pltpu.make_async_copy(src.at[0], dst, load_sem.at[i])
        for i, (src, dst) in enumerate(
            (
                (leaf_inv_hbm, leaf_inv),
                (leaf_upd_hbm, leaf_upd),
                (inner_upd_hbm, inner_upd),
                (inner_inv_hbm, inner_inv),
            )
        )
    ]
    for load in loads:
        load.start()

    barrier = pltpu.get_barrier_semaphore()

    def greet_front(i, carry):
        pl.semaphore_signal(
            barrier, inc=1, device_id=(x, lax.rem(m + i, fronts)), device_id_type=MESH
        )
        return carry

    lax.fori_loop(1, fronts, greet_front, 0)
    for i in range(1, leaves):
        pl.semaphore_signal(
            barrier, inc=1, device_id=(lax.rem(x + i, leaves), m), device_id_type=MESH
        )

    seeds = jnp.zeros((probes, 1), jnp.int32)
    row = lax.broadcasted_iota(jnp.int32, (probes, 1), 0)
    for p in range(probes):
        seeds = jnp.where(row == p, seeds_ref[p], seeds)

    piece = 512

    def make_signs(i, carry):
        start = pl.multiple_of(i * piece, piece)
        z = probe_signs(seeds, x, columns, start, (probes, piece))
        signs[:, pl.ds(start, piece)] = z.astype(bf16)
        return carry

    lax.fori_loop(0, columns // piece, make_signs, 0)
    own_signs = probe_signs(seeds, x + 1 + leaves, columns, m * width, (probes, width))

    pl.semaphore_wait(barrier, fronts - 1 + leaves - 1)

    map_copies = []
    for i in range(1, leaves):
        copy = pltpu.make_async_remote_copy(
            src_ref=maps_ref.at[0],
            dst_ref=all_maps.at[x],
            send_sem=map_send.at[i - 1],
            recv_sem=map_recv.at[i - 1],
            device_id=(lax.rem(x + i, leaves), m),
            device_id_type=MESH,
        )
        copy.start()
        map_copies.append(copy)
    all_maps[x] = maps_ref[0]

    def rows_times(vector, matrix):
        return lax.dot_general(vector, matrix, NT, preferred_element_type=f32)

    loads[0].wait()
    y_leaf = rows_times(signs[...], leaf_inv[...])
    leaf_y[...] = y_leaf

    for copy in map_copies:
        copy.wait()

    blocks = columns // BLOCK
    count = all_maps.shape[2]
    slot_pair = all_maps[pl.ds((x // 2) * 2, 1)][0]
    slot_map = jnp.where(x % 2 == 0, slot_pair[0:1], slot_pair[1:2])
    root_pair = all_maps[1]
    root_map = jnp.where(x // 2 == 0, root_pair[0:1], root_pair[1:2])
    target = lax.broadcasted_iota(jnp.int32, (blocks, count), 0)
    source = lax.broadcasted_iota(jnp.int32, (blocks, count), 1) + 1

    def find(values, wanted):
        return jnp.max(jnp.where(values == wanted, source, 0), axis=1, keepdims=True)

    direct = find(slot_map, target)
    inner = find(root_map, target)
    through = find(slot_map, jnp.where(inner == 0, -1, inner + (blocks - 1)))
    lane = lax.broadcasted_iota(jnp.int32, (blocks, 128), 1)
    sub = lax.broadcasted_iota(jnp.int32, (blocks, 128), 0)

    def as_row(column):
        return jnp.sum(jnp.where(lane == sub, column, 0), axis=0, keepdims=True)

    table_v[...] = jnp.zeros((8, 128), jnp.int32)
    table_v[0:1, :] = as_row(direct)
    table_v[1:2, :] = as_row(through)
    table_v[2:3, :] = as_row(inner)
    table_copy = pltpu.make_async_copy(table_v, table_s, table_sem)
    table_copy.start()
    table_copy.wait()

    def pick_columns(matrix, table, out):
        left_half = lax.broadcasted_iota(jnp.int32, (width, 128), 1) < BLOCK

        def half(entry, side):
            block = jnp.maximum(entry - 1, 0)
            at = (block >> 1) * 128
            tile = matrix[:, pl.ds(at, 128)].astype(f32)
            turned = pltpu.roll(tile, BLOCK, 1)
            odd = jnp.full((width, 128), block & 1, jnp.int32)
            found = jnp.full((width, 128), entry, jnp.int32)
            here = jnp.where(odd == side, tile, turned)
            return jnp.where(found > 0, here, 0.0)

        def body(j, carry):
            first = half(table_s[table, 2 * j], 0)
            second = half(table_s[table, 2 * j + 1], 1)
            at = pl.multiple_of(j * 128, 128)
            out[:, pl.ds(at, 128)] = jnp.where(left_half, first, second).astype(bf16)
            return carry

        lax.fori_loop(0, blocks // 2, body, 0, unroll=2)

    def sum_start(which, vector, matrix, more=None):
        partial = jnp.dot(vector, matrix[...], preferred_element_type=f32)
        if more is not None:
            partial = partial + more
        for j in range(fronts):
            send_part[which, j] = partial[:, j * width : (j + 1) * width].astype(bf16)
        recv_part[which, m] = send_part[which, m]

        def send(i, carry):
            j = lax.rem(m + i, fronts)
            pltpu.make_async_remote_copy(
                src_ref=send_part.at[which, j],
                dst_ref=recv_part.at[which, m],
                send_sem=part_send.at[which],
                recv_sem=part_recv.at[which],
                device_id=(x, j),
                device_id_type=MESH,
            ).start()
            return carry

        lax.fori_loop(1, fronts, send, 0)

    def wait_for(buffer, sem):
        part = buffer.at[pl.ds(0, fronts - 1)]
        pltpu.make_async_copy(part, part, sem).wait()

    def sum_finish(which):
        wait_for(recv_part.at[which], part_recv.at[which])
        total = recv_part[which, 0].astype(f32)
        for j in range(1, fronts):
            total = total + recv_part[which, j].astype(f32)
        return total

    def share_start(which, chunk_ref):
        def send(i, carry):
            j = lax.rem(m + i, fronts)
            pltpu.make_async_remote_copy(
                src_ref=chunk_ref,
                dst_ref=recv_all.at[which, m],
                send_sem=all_send.at[which],
                recv_sem=all_recv.at[which],
                device_id=(x, j),
                device_id_type=MESH,
            ).start()
            return carry

        lax.fori_loop(1, fronts, send, 0)
        recv_all[which, m] = chunk_ref[...]

    def share_finish(which):
        wait_for(recv_all.at[which], all_recv.at[which])
        return jnp.concatenate([recv_all[which, j] for j in range(fronts)], axis=1)

    def hop(src, dst, send_sem, recv_sem, to):
        return pltpu.make_async_remote_copy(
            src_ref=src,
            dst_ref=dst,
            send_sem=send_sem,
            recv_sem=recv_sem,
            device_id=(to, m),
            device_id_type=MESH,
        )

    LEAF_SUM, ROOT_SUM, BACK_SUM, LAST_SUM = 0, 1, 2, 3
    RESIDUAL, ROOT_X, SLOT_X = 0, 1, 2

    yb_leaf = y_leaf.astype(bf16)
    loads[1].wait()
    pick_columns(leaf_upd, 0, to_slot)
    sum_start(LEAF_SUM, yb_leaf, to_slot)
    pick_columns(leaf_upd, 1, to_root)

    hop_up_copy = hop(hop_send.at[0], hop_up, hop_send_sem.at[0], hop_up_sem, jnp.maximum(x - 1, 0))
    root_copy = hop(hop_send.at[1], hop_root.at[x], hop_send_sem.at[1], hop_root_sem.at[x], 1)

    def send_to_root():
        hop_send[1] = sum_finish(ROOT_SUM)
        root_copy.start()

    @pl.when(jnp.logical_not(is_slot))
    def _():
        hop_send[0] = sum_finish(LEAF_SUM)
        hop_up_copy.start()
        sum_start(ROOT_SUM, yb_leaf, to_root)
        loads[2].wait()
        loads[3].wait()

    @pl.when(is_slot)
    def _():
        own_sum = sum_finish(LEAF_SUM)
        hop_up_copy.wait_recv()
        own_chunk[RESIDUAL] = (own_signs - (own_sum + hop_up[...])).astype(bf16)
        share_start(RESIDUAL, own_chunk.at[RESIDUAL])
        loads[2].wait()
        pick_columns(inner_upd, 2, slot_root)
        carried = jnp.dot(yb_leaf, to_root[...], preferred_element_type=f32)
        loads[3].wait()
        y_slot = rows_times(share_finish(RESIDUAL), inner_inv[...])
        sum_start(ROOT_SUM, y_slot.astype(bf16), slot_root, carried)
        leaf_v[...] = y_slot
        send_to_root()

    @pl.when(x == 3)
    def _():
        send_to_root()

    @pl.when(is_root)
    def _():
        total = sum_finish(ROOT_SUM)
        for other in (0, 2, 3):
            hop(hop_send.at[1], hop_root.at[other], hop_send_sem.at[1], hop_root_sem.at[other], 1).wait_recv()
            total = total + hop_root[other]
        own_chunk[RESIDUAL] = (own_signs - total).astype(bf16)
        share_start(RESIDUAL, own_chunk.at[RESIDUAL])
        y_root = rows_times(share_finish(RESIDUAL), inner_inv[...])
        sum_start(BACK_SUM, y_root.astype(bf16), inner_inv)
        result = sum_finish(BACK_SUM)
        own_chunk[ROOT_X] = result.astype(bf16)
        for i, other in enumerate((0, 2, 3)):
            hop(own_chunk.at[ROOT_X], hop_chunk.at[0], hop_send_sem.at[2 + i], hop_chunk_sem.at[0], other).start()
        share_start(ROOT_X, own_chunk.at[ROOT_X])
        inner_out[0] = result

    @pl.when(jnp.logical_not(is_root))
    def _():
        hop(own_chunk.at[ROOT_X], hop_chunk.at[0], hop_send_sem.at[2], hop_chunk_sem.at[0], 1).wait_recv()
        share_start(ROOT_X, hop_chunk.at[0])

    x_root = share_finish(ROOT_X)

    @pl.when(is_slot)
    def _():
        v = rows_times(x_root, slot_root[...])
        s = (leaf_v[...] - v).astype(bf16)
        sum_start(BACK_SUM, s, inner_inv)

    leaf_v[...] = rows_times(x_root, to_root[...])

    @pl.when(is_slot)
    def _():
        result = sum_finish(BACK_SUM)
        own_chunk[SLOT_X] = result.astype(bf16)
        hop(own_chunk.at[SLOT_X], hop_chunk.at[1], hop_send_sem.at[2], hop_chunk_sem.at[1], x + 1).start()
        share_start(SLOT_X, own_chunk.at[SLOT_X])
        inner_out[0] = result

    @pl.when(jnp.logical_not(is_slot))
    def _():
        hop(own_chunk.at[SLOT_X], hop_chunk.at[1], hop_send_sem.at[5], hop_chunk_sem.at[1], x - 1).wait_recv()
        share_start(SLOT_X, hop_chunk.at[1])

    @pl.when(x == 3)
    def _():
        inner_out[0] = jnp.zeros((probes, width), f32)

    x_slot = share_finish(SLOT_X)
    v = rows_times(x_slot, to_slot[...]) + leaf_v[...]
    s = (leaf_y[...] - v).astype(bf16)
    sum_start(LAST_SUM, s, leaf_inv)
    leaf_out[0] = sum_finish(LAST_SUM)

    for which in (LEAF_SUM, ROOT_SUM, LAST_SUM):
        wait_for(send_part.at[which], part_send.at[which])
    for which in (ROOT_X, SLOT_X):
        wait_for(recv_all.at[which], all_send.at[which])

    @pl.when(x != 3)
    def _():
        wait_for(send_part.at[BACK_SUM], part_send.at[BACK_SUM])
        wait_for(recv_all.at[RESIDUAL], all_send.at[RESIDUAL])

    @pl.when(jnp.logical_not(is_slot))
    def _():
        hop_up_copy.wait_send()

    @pl.when(jnp.logical_not(is_root))
    def _():
        root_copy.wait_send()

    @pl.when(is_slot)
    def _():
        hop(own_chunk.at[SLOT_X], hop_chunk.at[1], hop_send_sem.at[2], hop_chunk_sem.at[1], x + 1).wait_send()

    @pl.when(is_root)
    def _():
        for i, other in enumerate((0, 2, 3)):
            hop(own_chunk.at[ROOT_X], hop_chunk.at[0], hop_send_sem.at[2 + i], hop_chunk_sem.at[0], other).wait_send()


def shards(probe_seeds, leaf_inverse, leaf_update, internal_inverse, internal_update, child_map):
    fronts = lax.axis_size("front")
    leaves = lax.axis_size("leaf")
    probes = probe_seeds.shape[0]
    width, columns = leaf_inverse.shape[1:]
    rows = leaf_update.shape[2]
    f32, bf16 = jnp.float32, jnp.bfloat16
    dma = pltpu.SemaphoreType.DMA
    vmem = pl.BlockSpec(memory_space=pltpu.VMEM)
    hbm = pl.BlockSpec(memory_space=pl.ANY)
    out = jax.ShapeDtypeStruct((1, probes, width), f32)
    return pl.pallas_call(
        functools.partial(kernel, fronts, probes, columns, width),
        out_shape=(out, out),
        in_specs=[pl.BlockSpec(memory_space=pltpu.SMEM), vmem, hbm, hbm, hbm, hbm],
        out_specs=(vmem, vmem),
        scratch_shapes=[
            pltpu.VMEM((width, columns), bf16),
            pltpu.VMEM((width, rows), bf16),
            pltpu.VMEM((width, columns), bf16),
            pltpu.VMEM((width, rows), bf16),
            pltpu.VMEM((width, columns), bf16),
            pltpu.VMEM((width, columns), bf16),
            pltpu.VMEM((width, columns), bf16),
            pltpu.VMEM((probes, columns), bf16),
            pltpu.VMEM((leaves, *child_map.shape[1:]), jnp.int32),
            pltpu.VMEM((8, 128), jnp.int32),
            pltpu.SMEM((8, 128), jnp.int32),
            pltpu.VMEM((4, fronts, probes, width), bf16),
            pltpu.VMEM((4, fronts, probes, width), bf16),
            pltpu.VMEM((3, probes, width), bf16),
            pltpu.VMEM((3, fronts, probes, width), bf16),
            pltpu.VMEM((2, probes, width), f32),
            pltpu.VMEM((probes, width), f32),
            pltpu.VMEM((leaves, probes, width), f32),
            pltpu.VMEM((2, probes, width), bf16),
            pltpu.VMEM((probes, width), f32),
            pltpu.VMEM((probes, width), f32),
            dma((4,)),
            dma,
            dma((3,)),
            dma((3,)),
            dma((4,)),
            dma((4,)),
            dma((3,)),
            dma((3,)),
            dma((6,)),
            dma,
            dma((4,)),
            dma((2,)),
        ],
        compiler_params=pltpu.CompilerParams(
            collective_id=0, has_side_effects=True, vmem_limit_bytes=40 * 1024 * 1024
        ),
        name="solves",
    )(probe_seeds, child_map, leaf_inverse, leaf_update, internal_inverse, internal_update)


def solution(mesh):
    return jax.shard_map(
        shards,
        mesh=mesh,
        in_specs=(
            P(),
            P("leaf", "front", None),
            P("leaf", "front", None),
            P("leaf", "front", None),
            P("leaf", "front", None),
            P("leaf", None, None),
        ),
        out_specs=(P("leaf", None, "front"), P("leaf", None, "front")),
        check_vma=False,
    )
```

```python
import functools

import jax
import jax.numpy as jnp
from jax import lax
from jax.experimental import pallas as pl
from jax.experimental.pallas import tpu as pltpu
from jax.sharding import PartitionSpec as P

BLOCK = 64
MOD = 32749
MESH = pl.DeviceIdType.MESH
NT = (((1,), (1,)), ((), ()))
OFFSETS = (
    (2, 2), (2, 1), (1, 2), (2, 3), (3, 2), (2, 0), (0, 2), (1, 1),
    (3, 3), (1, 3), (3, 1), (1, 0), (0, 1), (3, 0), (0, 3), (0, 0),
)


def packed(values):
    word = sum(v << (2 * i) for i, v in enumerate(values))
    return word - (1 << 32) if word >= 1 << 31 else word


OFFSET_Z = packed([z for z, _ in OFFSETS])
OFFSET_Y = packed([y for _, y in OFFSETS])


def mod_prime(x):
    q = (x.astype(jnp.float32) * (1.0 / MOD)).astype(jnp.int32)
    r = x - q * MOD
    r = jnp.where(r < 0, r + MOD, r)
    return jnp.where(r >= MOD, r - MOD, r)


def probe_signs(seeds, node_id, columns, start, shape):
    index = node_id * columns + start + lax.broadcasted_iota(jnp.int32, shape, 1)
    wrapped = index >= MOD
    lower = jnp.where(wrapped, index - MOD, index)
    upper = jnp.where(wrapped, 1, 0)
    hashed = mod_prime(lower * 30011 + upper * 7717 + seeds)
    hashed = mod_prime(hashed * hashed)
    hashed = mod_prime(hashed * 21143 + lower)
    hashed = mod_prime(hashed * hashed + upper)
    return (1 - 2 * ((hashed >> 3) & 1)).astype(jnp.float32)


def kernel(
    fronts,
    probes,
    columns,
    width,
    seeds_hbm,
    maps_hbm,
    leaf_inv_hbm,
    leaf_upd_hbm,
    inner_inv_hbm,
    inner_upd_hbm,
    leaf_hbm,
    inner_hbm,
    seeds_s,
    leaf_inv,
    leaf_upd,
    inner_inv,
    inner_upd,
    to_slot,
    to_root,
    slot_root,
    root_inv,
    signs,
    leaf_all,
    carried,
    all_maps,
    table_v,
    table_s,
    send_part,
    recv_part,
    own_chunk,
    recv_all,
    hop_send,
    hop_up,
    hop_root,
    hop_root_x,
    hop_slot_x,
    leaf_y,
    inner_y,
    leaf_v,
    leaf_out,
    inner_out,
    load_sem,
    small_sem,
    map_send,
    map_recv,
    part_send,
    part_recv,
    all_send,
    all_recv,
    hop_up_send,
    hop_up_recv,
    hop_root_send,
    hop_root_recv,
    hop_x_send,
    hop_x_recv,
    bulk_send,
    bulk_recv,
    out_sem,
):
    x = lax.axis_index("leaf")
    m = lax.axis_index("front")
    m_z, m_y, m_c = m // 8, lax.rem(m // 2, 4), lax.rem(m, 2)
    leaves = 4
    f32, bf16 = jnp.float32, jnp.bfloat16
    is_slot = (x == 0) | (x == 2)
    is_root = x == 1
    part_rows = probes // 2
    halves = (0, 1)

    def rows_of(h):
        return pl.ds(h * part_rows, part_rows)

    seed_copy = pltpu.make_async_copy(seeds_hbm, seeds_s, small_sem.at[0])
    map_copy = pltpu.make_async_copy(maps_hbm.at[0], all_maps.at[x], small_sem.at[1])
    seed_copy.start()
    map_copy.start()
    loads = [
        pltpu.make_async_copy(src.at[0], dst, load_sem.at[i])
        for i, (src, dst) in enumerate(
            (
                (leaf_inv_hbm, leaf_inv),
                (leaf_upd_hbm, leaf_upd),
                (inner_upd_hbm, inner_upd),
                (inner_inv_hbm, inner_inv),
            )
        )
    ]
    loads[0].start()
    loads[1].start()

    def peer(i):
        at = (i // 2) * 2
        z = lax.rem(m_z + ((jnp.int32(OFFSET_Z) >> at) & 3), 4)
        y = lax.rem(m_y + ((jnp.int32(OFFSET_Y) >> at) & 3), 4)
        return z * 8 + y * 2 + lax.rem(m_c + 1 + i, 2)

    barrier = pltpu.get_barrier_semaphore()

    def greet_front(i, carry):
        pl.semaphore_signal(barrier, inc=1, device_id=(x, peer(i)), device_id_type=MESH)
        return carry

    lax.fori_loop(0, fronts - 1, greet_front, 0)
    for i in range(1, leaves):
        pl.semaphore_signal(
            barrier, inc=1, device_id=(lax.rem(x + i, leaves), m), device_id_type=MESH
        )

    ROOT_AT = 1

    def map_to(to, kind):
        return pltpu.make_async_remote_copy(
            src_ref=maps_hbm.at[0],
            dst_ref=all_maps.at[x],
            send_sem=map_send.at[to],
            recv_sem=map_recv.at[kind],
            device_id=(to, m),
            device_id_type=MESH,
        )

    def slot_map_copy(to):
        return pltpu.make_async_remote_copy(
            src_ref=maps_hbm.at[0],
            dst_ref=all_maps.at[x],
            send_sem=map_send.at[0],
            recv_sem=map_recv.at[0],
            device_id=(to, m),
            device_id_type=MESH,
        )

    bulk_rows = width // 4

    def bulk_copy(piece, to):
        rows = pl.ds(piece * bulk_rows, bulk_rows)
        return pltpu.make_async_remote_copy(
            src_ref=inner_inv_hbm.at[0, rows],
            dst_ref=root_inv.at[rows],
            send_sem=bulk_send.at[to // 2],
            recv_sem=bulk_recv,
            device_id=(to, m),
            device_id_type=MESH,
        )

    greeted = fronts - 1 + leaves - 1

    @pl.when(is_slot)
    def _():
        pl.semaphore_wait(barrier, greeted)
        slot_map_copy(x + 1).start()

    seed_copy.wait()
    seeds = jnp.zeros((probes, 1), jnp.int32)
    row = lax.broadcasted_iota(jnp.int32, (probes, 1), 0)
    for p in range(probes):
        seeds = jnp.where(row == p, seeds_s[p], seeds)

    piece = 512

    def make_signs(i, carry):
        start = pl.multiple_of(i * piece, piece)
        z = probe_signs(seeds, x, columns, start, (probes, piece))
        signs[:, pl.ds(start, piece)] = z.astype(bf16)
        return carry

    lax.fori_loop(0, columns // piece, make_signs, 0)

    def rows_times(vector, matrix):
        return lax.dot_general(vector, matrix[...], NT, preferred_element_type=f32)

    loads[0].wait()
    leaf_y[...] = rows_times(signs[...], leaf_inv)
    yb_leaf = leaf_y[...].astype(bf16)
    loads[1].wait()
    loads[2].start()
    loads[3].start()
    wide = 2048

    def leaf_products(i, carry):
        at = pl.ds(pl.multiple_of(i * wide, wide), wide)
        leaf_all[:, at] = jnp.dot(
            yb_leaf, leaf_upd[:, at], preferred_element_type=f32
        ).astype(bf16)
        return carry

    lax.fori_loop(0, leaf_upd.shape[1] // wide, leaf_products, 0)
    map_copy.wait()

    @pl.when(jnp.logical_not(is_slot))
    def _():
        pl.semaphore_wait(barrier, greeted)

    @pl.when(is_root)
    def _():
        for to in (0, 2, 3):
            map_to(to, 1).start()
        bulk_copy(0, 0).start()
        for q in range(4):
            bulk_copy(q, 2).start()

    blocks = columns // BLOCK
    count = all_maps.shape[2]
    target = lax.broadcasted_iota(jnp.int32, (blocks, count), 0)
    source = lax.broadcasted_iota(jnp.int32, (blocks, count), 1) + 1
    lane = lax.broadcasted_iota(jnp.int32, (blocks, 128), 1)
    sub = lax.broadcasted_iota(jnp.int32, (blocks, 128), 0)

    def find(values, wanted):
        return jnp.max(jnp.where(values == wanted, source, 0), axis=1, keepdims=True)

    def as_row(column):
        return jnp.sum(jnp.where(lane == sub, column, 0), axis=0, keepdims=True)

    def slot_map():
        pair = all_maps[pl.ds((x // 2) * 2, 1)][0]
        return jnp.where(x % 2 == 0, pair[0:1], pair[1:2])

    def table_out(which):
        copy = pltpu.make_async_copy(table_v.at[which], table_s.at[which], small_sem.at[2])
        copy.start()
        copy.wait()

    table_v[...] = jnp.zeros(table_v.shape, jnp.int32)

    @pl.when(jnp.logical_not(is_slot))
    def _():
        slot_map_copy(x).wait_recv()

    table_v[0, 0:1, :] = as_row(find(slot_map(), target))
    table_out(0)

    def pick(read, table, at, rows, write):
        left_half = lax.broadcasted_iota(jnp.int32, (rows, 128), 1) < BLOCK

        def half(entry, side):
            block = jnp.maximum(entry - 1, 0)
            odd = jnp.full((rows, 128), block & 1, jnp.int32)
            found = jnp.full((rows, 128), entry, jnp.int32)
            tile = read((block >> 1) * 128).astype(f32)
            turned = pltpu.roll(tile, BLOCK, 1)
            here = jnp.where(odd == side, tile, turned)
            return jnp.where(found > 0, here, 0.0)

        def body(j, carry):
            first = half(table_s[table, at, 2 * j], 0)
            second = half(table_s[table, at, 2 * j + 1], 1)
            write(j, jnp.where(left_half, first, second).astype(bf16))
            return carry

        lax.fori_loop(0, blocks // 2, body, 0, unroll=4)

    def pick_matrix(matrix, table, at, out):
        def write(j, tile):
            out[:, pl.ds(pl.multiple_of(j * 128, 128), 128)] = tile

        pick(lambda start: matrix[:, pl.ds(start, 128)], table, at, width, write)

    def pick_products(table, at, write):
        pick(lambda start: leaf_all[:, pl.ds(start, 128)], table, at, probes, write)

    def to_peers(src, dst, send_sem, recv_sem):
        def send(i, carry):
            j = peer(i)
            pltpu.make_async_remote_copy(
                src_ref=src(j),
                dst_ref=dst,
                send_sem=send_sem,
                recv_sem=recv_sem,
                device_id=(x, j),
                device_id_type=MESH,
            ).start()
            return carry

        lax.fori_loop(0, fronts - 1, send, 0)

    def wait_for(buffer, sem):
        part = buffer.at[pl.ds(0, fronts - 1)]
        pltpu.make_async_copy(part, part, sem).wait()

    def parts_start(which, h):
        to_peers(
            lambda j: send_part.at[which, h, j],
            recv_part.at[which, h, m],
            part_send.at[which, h],
            part_recv.at[which, h],
        )
        recv_part[which, h, m] = send_part[which, h, m]

    def sum_start(which, h, vector, matrix, more=None):
        partial = jnp.dot(vector, matrix[...], preferred_element_type=f32)
        for j in range(fronts):
            chunk = partial[:, j * width : (j + 1) * width]
            if more is not None:
                chunk = chunk + more[h, j].astype(f32)
            send_part[which, h, j] = chunk.astype(bf16)
        parts_start(which, h)

    def sum_finish(which, h):
        wait_for(recv_part.at[which, h], part_recv.at[which, h])
        sums = []
        for q in range(4):
            total = recv_part[which, h, q].astype(f32)
            for j in range(q + 4, fronts, 4):
                total = total + recv_part[which, h, j].astype(f32)
            sums.append(total)
        return (sums[0] + sums[1]) + (sums[2] + sums[3])

    def share_start(which, h, chunk_ref):
        to_peers(
            lambda j: chunk_ref,
            recv_all.at[which, h, m],
            all_send.at[which, h],
            all_recv.at[which, h],
        )
        recv_all[which, h, m] = chunk_ref[...]

    def share_finish(which, h):
        wait_for(recv_all.at[which, h], all_recv.at[which, h])
        return jnp.concatenate([recv_all[which, h, j] for j in range(fronts)], axis=1)

    def hop(src, dst, send_sem, recv_sem, to):
        return pltpu.make_async_remote_copy(
            src_ref=src,
            dst_ref=dst,
            send_sem=send_sem,
            recv_sem=recv_sem,
            device_id=(to, m),
            device_id_type=MESH,
        )

    LEAF_SUM, ROOT_SUM, ROOT_BACK, SLOT_BACK, LAST_SUM = 0, 1, 2, 3, 4
    SLOT_RHS, ROOT_RHS, ROOT_X, SLOT_X = 0, 1, 2, 3

    def up_copy(h, to):
        return hop(hop_send.at[0, h], hop_up.at[h], hop_up_send.at[h], hop_up_recv.at[h], to)

    def root_copy(h, i, origin, to):
        return hop(
            hop_root.at[origin, h], hop_root.at[origin, h], hop_root_send.at[i, h], hop_root_recv.at[origin, h], to
        )

    def root_x_copy(h, to):
        return hop(hop_send.at[1, h], hop_root_x.at[h], hop_x_send.at[0, h], hop_x_recv.at[0, h], to)

    def slot_x_copy(h, to):
        return hop(own_chunk.at[SLOT_X, h], hop_slot_x.at[h], hop_x_send.at[1, h], hop_x_recv.at[1, h], to)

    def half_of(value, h):
        return value[h * part_rows : (h + 1) * part_rows]

    def write_leaf_part(j, tile):
        for h in halves:
            send_part[LEAF_SUM, h, j] = tile[h * part_rows : (h + 1) * part_rows]

    pick_products(0, 0, write_leaf_part)
    for h in halves:
        parts_start(LEAF_SUM, h)

    @pl.when(jnp.logical_not(is_root))
    def _():
        map_to(0, 1).wait_recv()

    root_pair = all_maps[1]
    root_map = jnp.where(x // 2 == 0, root_pair[0:1], root_pair[1:2])
    inner = find(root_map, target)
    through = find(slot_map(), jnp.where(inner == 0, -1, inner + (blocks - 1)))
    table_v[1, 0:1, :] = as_row(through)
    table_v[1, 1:2, :] = as_row(inner)
    table_out(1)

    @pl.when(jnp.logical_not(is_slot))
    def _():
        for h in halves:
            hop_send[0, h] = sum_finish(LEAF_SUM, h)
            up_copy(h, x - 1).start()

        @pl.when(is_root)
        def _():
            for q in range(1, 4):
                bulk_copy(q, 0).start()

        def write_root_part(j, tile):
            for h in halves:
                send_part[ROOT_SUM, h, j] = half_of(tile, h)

        pick_products(1, 0, write_root_part)
        for h in halves:
            parts_start(ROOT_SUM, h)
        loads[2].wait()
        loads[3].wait()
        pick_matrix(leaf_upd, 0, 0, to_slot)
        pick_matrix(leaf_upd, 1, 0, to_root)
        for h in halves:
            hop_root[x, h] = sum_finish(ROOT_SUM, h)
            for i, to in enumerate((0, 2)):
                root_copy(h, i, x, to).start()

    @pl.when(is_slot)
    def _():
        def write_carried(j, tile):
            for h in halves:
                carried[h, j] = half_of(tile, h)

        pick_products(1, 0, write_carried)
        loads[2].wait()
        pick_matrix(inner_upd, 1, 1, slot_root)
        slot_signs = probe_signs(seeds, x + 1 + leaves, columns, m * width, (probes, width))
        root_signs = probe_signs(seeds, ROOT_AT + 1 + leaves, columns, m * width, (probes, width))
        loads[3].wait()
        for h in halves:
            own_sum = sum_finish(LEAF_SUM, h)
            up_copy(h, x).wait_recv()
            own_chunk[SLOT_RHS, h] = (half_of(slot_signs, h) - (own_sum + hop_up[h])).astype(bf16)
            share_start(SLOT_RHS, h, own_chunk.at[SLOT_RHS, h])
        pick_matrix(leaf_upd, 0, 0, to_slot)
        for h in halves:
            y_slot = rows_times(share_finish(SLOT_RHS, h), inner_inv)
            inner_y[rows_of(h)] = y_slot
            sum_start(ROOT_SUM, h, y_slot.astype(bf16), slot_root, carried)
        pick_matrix(leaf_upd, 1, 0, to_root)
        for h in halves:
            hop_root[x, h] = sum_finish(ROOT_SUM, h)
            root_copy(h, 0, x, 2 - x).start()
        for h in halves:
            for origin in (1, 3):
                root_copy(h, 0, origin, x).wait_recv()
            root_copy(h, 0, 2 - x, x).wait_recv()
            total = (hop_root[0, h] + hop_root[1, h]) + (hop_root[2, h] + hop_root[3, h])
            own_chunk[ROOT_RHS, h] = (half_of(root_signs, h) - total).astype(bf16)
            share_start(ROOT_RHS, h, own_chunk.at[ROOT_RHS, h])
        pltpu.make_async_copy(root_inv, root_inv, bulk_recv).wait()
        for h in halves:
            y_root = rows_times(share_finish(ROOT_RHS, h), root_inv)
            sum_start(ROOT_BACK, h, y_root.astype(bf16), root_inv)
        for h in halves:
            result = sum_finish(ROOT_BACK, h)
            own_chunk[ROOT_X, h] = result.astype(bf16)
            hop_send[1, h] = result
            root_x_copy(h, x + 1).start()
            share_start(ROOT_X, h, own_chunk.at[ROOT_X, h])
        for h in halves:
            x_root = share_finish(ROOT_X, h)
            s = (inner_y[rows_of(h)] - rows_times(x_root, slot_root)).astype(bf16)
            sum_start(SLOT_BACK, h, s, inner_inv)
        for h in halves:
            x_root = jnp.concatenate([recv_all[ROOT_X, h, j] for j in range(fronts)], axis=1)
            leaf_v[rows_of(h)] = leaf_y[rows_of(h)] - rows_times(x_root, to_root)
        for h in halves:
            result = sum_finish(SLOT_BACK, h)
            own_chunk[SLOT_X, h] = result.astype(bf16)
            slot_x_copy(h, x + 1).start()
            share_start(SLOT_X, h, own_chunk.at[SLOT_X, h])
            inner_out[rows_of(h)] = result

    @pl.when(jnp.logical_not(is_slot))
    def _():
        for h in halves:
            root_x_copy(h, x).wait_recv()
            own_chunk[ROOT_X, h] = hop_root_x[h].astype(bf16)
            share_start(ROOT_X, h, own_chunk.at[ROOT_X, h])
            inner_out[rows_of(h)] = jnp.where(is_root, hop_root_x[h], 0.0)
        for h in halves:
            x_root = share_finish(ROOT_X, h)
            leaf_v[rows_of(h)] = leaf_y[rows_of(h)] - rows_times(x_root, to_root)
        for h in halves:
            slot_x_copy(h, x).wait_recv()
            share_start(SLOT_X, h, hop_slot_x.at[h])

    for h in halves:
        x_slot = share_finish(SLOT_X, h)
        s = (leaf_v[rows_of(h)] - rows_times(x_slot, to_slot)).astype(bf16)
        sum_start(LAST_SUM, h, s, leaf_inv)
    inner_write = pltpu.make_async_copy(inner_out, inner_hbm.at[0], out_sem.at[2])
    inner_write.start()
    leaf_writes = [
        pltpu.make_async_copy(leaf_out.at[rows_of(h)], leaf_hbm.at[0, rows_of(h)], out_sem.at[h])
        for h in halves
    ]
    for h in halves:
        leaf_out[rows_of(h)] = sum_finish(LAST_SUM, h)
        leaf_writes[h].start()

    for h in halves:
        for which in (LEAF_SUM, ROOT_SUM, LAST_SUM):
            wait_for(send_part.at[which, h], part_send.at[which, h])
        for which in (ROOT_X, SLOT_X):
            wait_for(recv_all.at[which, h], all_send.at[which, h])

    @pl.when(is_slot)
    def _():
        slot_map_copy(x + 1).wait_send()
        for h in halves:
            for which in (ROOT_BACK, SLOT_BACK):
                wait_for(send_part.at[which, h], part_send.at[which, h])
            for which in (SLOT_RHS, ROOT_RHS):
                wait_for(recv_all.at[which, h], all_send.at[which, h])
            root_copy(h, 0, x, 2 - x).wait_send()
            root_x_copy(h, x + 1).wait_send()
            slot_x_copy(h, x + 1).wait_send()

    @pl.when(jnp.logical_not(is_slot))
    def _():
        for h in halves:
            up_copy(h, x - 1).wait_send()
            for i, to in enumerate((0, 2)):
                root_copy(h, i, x, to).wait_send()

    @pl.when(is_root)
    def _():
        for to in (0, 2, 3):
            map_to(to, 1).wait_send()
        for to in (0, 2):
            pltpu.make_async_copy(root_inv, root_inv, bulk_send.at[to // 2]).wait()

    inner_write.wait()
    for copy in leaf_writes:
        copy.wait()


def write_out(leaf_ref, inner_ref, leaf_hbm, inner_hbm, sem):
    copies = [
        pltpu.make_async_copy(leaf_ref, leaf_hbm, sem.at[0]),
        pltpu.make_async_copy(inner_ref, inner_hbm, sem.at[1]),
    ]
    for copy in copies:
        copy.start()
    for copy in copies:
        copy.wait()


def shards(probe_seeds, leaf_inverse, leaf_update, internal_inverse, internal_update, child_map):
    fronts = lax.axis_size("front")
    leaves = lax.axis_size("leaf")
    probes = probe_seeds.shape[0]
    width, columns = leaf_inverse.shape[1:]
    rows = leaf_update.shape[2]
    f32, bf16 = jnp.float32, jnp.bfloat16
    dma = pltpu.SemaphoreType.DMA
    hbm = pl.BlockSpec(memory_space=pltpu.HBM)
    out = jax.ShapeDtypeStruct((1, probes, width), f32)
    part = (probes // 2, width)
    leaf_part, inner_part = pl.pallas_call(
        functools.partial(kernel, fronts, probes, columns, width),
        out_shape=(out, out),
        in_specs=[hbm] * 6,
        out_specs=(hbm, hbm),
        scratch_shapes=[
            pltpu.SMEM((probes,), jnp.int32),
            pltpu.VMEM((width, columns), bf16),
            pltpu.VMEM((width, rows), bf16),
            pltpu.VMEM((width, columns), bf16),
            pltpu.VMEM((width, rows), bf16),
            pltpu.VMEM((width, columns), bf16),
            pltpu.VMEM((width, columns), bf16),
            pltpu.VMEM((width, columns), bf16),
            pltpu.VMEM((width, columns), bf16),
            pltpu.VMEM((probes, columns), bf16),
            pltpu.VMEM((probes, rows), bf16),
            pltpu.VMEM((2, fronts, *part), bf16),
            pltpu.VMEM((leaves, *child_map.shape[1:]), jnp.int32),
            pltpu.VMEM((2, 8, 128), jnp.int32),
            pltpu.SMEM((2, 8, 128), jnp.int32),
            pltpu.VMEM((5, 2, fronts, *part), bf16),
            pltpu.VMEM((5, 2, fronts, *part), bf16),
            pltpu.VMEM((4, 2, *part), bf16),
            pltpu.VMEM((4, 2, fronts, *part), bf16),
            pltpu.VMEM((2, 2, *part), f32),
            pltpu.VMEM((2, *part), f32),
            pltpu.VMEM((leaves, 2, *part), f32),
            pltpu.VMEM((2, *part), f32),
            pltpu.VMEM((2, *part), bf16),
            pltpu.VMEM((probes, width), f32),
            pltpu.VMEM((probes, width), f32),
            pltpu.VMEM((probes, width), f32),
            pltpu.VMEM((probes, width), f32),
            pltpu.VMEM((probes, width), f32),
            dma((4,)),
            dma((3,)),
            dma((leaves,)),
            dma((2,)),
            dma((5, 2)),
            dma((5, 2)),
            dma((4, 2)),
            dma((4, 2)),
            dma((2,)),
            dma((2,)),
            dma((2, 2)),
            dma((leaves, 2)),
            dma((2, 2)),
            dma((2, 2)),
            dma((2,)),
            dma,
            dma((3,)),
        ],
        compiler_params=pltpu.CompilerParams(
            collective_id=0, has_side_effects=True, vmem_limit_bytes=60 * 1024 * 1024
        ),
        name="solves",
    )(probe_seeds, child_map, leaf_inverse, leaf_update, internal_inverse, internal_update)
    return pl.pallas_call(
        write_out,
        out_shape=(out, out),
        in_specs=[hbm, hbm],
        out_specs=(hbm, hbm),
        scratch_shapes=[dma((2,))],
        name="write_out",
    )(leaf_part, inner_part)


def solution(mesh):
    return jax.shard_map(
        shards,
        mesh=mesh,
        in_specs=(
            P(),
            P("leaf", "front", None),
            P("leaf", "front", None),
            P("leaf", "front", None),
            P("leaf", "front", None),
            P("leaf", None, None),
        ),
        out_specs=(P("leaf", None, "front"), P("leaf", None, "front")),
        check_vma=False,
    )
```

```python
import functools

import jax
import jax.numpy as jnp
from jax import lax
from jax.experimental import pallas as pl
from jax.experimental.pallas import tpu as pltpu
from jax.sharding import PartitionSpec as P

BLOCK = 64
MOD = 32749
MESH = pl.DeviceIdType.MESH
NT = (((1,), (1,)), ((), ()))
OFFSETS = (
    (2, 2), (2, 1), (1, 2), (2, 3), (3, 2), (2, 0), (0, 2), (1, 1),
    (3, 3), (1, 3), (3, 1), (1, 0), (0, 1), (3, 0), (0, 3), (0, 0),
)


def packed(values):
    word = sum(v << (2 * i) for i, v in enumerate(values))
    return word - (1 << 32) if word >= 1 << 31 else word


OFFSET_Z = packed([z for z, _ in OFFSETS])
OFFSET_Y = packed([y for _, y in OFFSETS])


def mod_prime(x):
    q = (x.astype(jnp.float32) * (1.0 / MOD)).astype(jnp.int32)
    r = x - q * MOD
    r = jnp.where(r < 0, r + MOD, r)
    return jnp.where(r >= MOD, r - MOD, r)


def probe_signs(seeds, node_id, columns, start, shape):
    index = node_id * columns + start + lax.broadcasted_iota(jnp.int32, shape, 1)
    wrapped = index >= MOD
    lower = jnp.where(wrapped, index - MOD, index)
    upper = jnp.where(wrapped, 1, 0)
    hashed = mod_prime(lower * 30011 + upper * 7717 + seeds)
    hashed = mod_prime(hashed * hashed)
    hashed = mod_prime(hashed * 21143 + lower)
    hashed = mod_prime(hashed * hashed + upper)
    return (1 - 2 * ((hashed >> 3) & 1)).astype(jnp.float32)


def kernel(
    fronts,
    probes,
    columns,
    width,
    seeds_hbm,
    maps_hbm,
    leaf_inv_hbm,
    leaf_upd_hbm,
    inner_inv_hbm,
    inner_upd_hbm,
    leaf_out,
    inner_out,
    seeds_s,
    leaf_inv,
    leaf_upd,
    inner_inv,
    inner_upd,
    to_slot,
    to_root,
    slot_root,
    root_inv,
    signs,
    leaf_all,
    carried,
    all_maps,
    table_v,
    table_s,
    send_part,
    recv_part,
    own_chunk,
    recv_all,
    hop_send,
    hop_up,
    hop_root,
    hop_root_x,
    hop_slot_x,
    leaf_y,
    inner_y,
    leaf_v,
    load_sem,
    small_sem,
    map_send,
    map_recv,
    part_send,
    part_recv,
    all_send,
    all_recv,
    hop_up_send,
    hop_up_recv,
    hop_root_send,
    hop_root_recv,
    hop_x_send,
    hop_x_recv,
    bulk_send,
    bulk_recv,
):
    x = lax.axis_index("leaf")
    m = lax.axis_index("front")
    m_z, m_y, m_c = m // 8, lax.rem(m // 2, 4), lax.rem(m, 2)
    leaves = 4
    f32, bf16 = jnp.float32, jnp.bfloat16
    is_slot = (x == 0) | (x == 2)
    is_root = x == 1
    part_rows = probes // 2
    halves = (0, 1)

    def rows_of(h):
        return pl.ds(h * part_rows, part_rows)

    seed_copy = pltpu.make_async_copy(seeds_hbm, seeds_s, small_sem.at[0])
    map_copy = pltpu.make_async_copy(maps_hbm.at[0], all_maps.at[x], small_sem.at[1])
    seed_copy.start()
    map_copy.start()
    loads = [
        pltpu.make_async_copy(src.at[0], dst, load_sem.at[i])
        for i, (src, dst) in enumerate(
            (
                (leaf_inv_hbm, leaf_inv),
                (leaf_upd_hbm, leaf_upd),
                (inner_upd_hbm, inner_upd),
                (inner_inv_hbm, inner_inv),
            )
        )
    ]
    loads[0].start()
    loads[1].start()

    def peer(i):
        at = (i // 2) * 2
        z = lax.rem(m_z + ((jnp.int32(OFFSET_Z) >> at) & 3), 4)
        y = lax.rem(m_y + ((jnp.int32(OFFSET_Y) >> at) & 3), 4)
        return z * 8 + y * 2 + lax.rem(m_c + 1 + i, 2)

    barrier = pltpu.get_barrier_semaphore()

    def greet_front(i, carry):
        pl.semaphore_signal(barrier, inc=1, device_id=(x, peer(i)), device_id_type=MESH)
        return carry

    lax.fori_loop(0, fronts - 1, greet_front, 0)
    for i in range(1, leaves):
        pl.semaphore_signal(
            barrier, inc=1, device_id=(lax.rem(x + i, leaves), m), device_id_type=MESH
        )

    ROOT_AT = 1

    def map_to(to, kind):
        return pltpu.make_async_remote_copy(
            src_ref=maps_hbm.at[0],
            dst_ref=all_maps.at[x],
            send_sem=map_send.at[to],
            recv_sem=map_recv.at[kind],
            device_id=(to, m),
            device_id_type=MESH,
        )

    def slot_map_copy(to):
        return pltpu.make_async_remote_copy(
            src_ref=maps_hbm.at[0],
            dst_ref=all_maps.at[x],
            send_sem=map_send.at[0],
            recv_sem=map_recv.at[0],
            device_id=(to, m),
            device_id_type=MESH,
        )

    pieces, early = 8, 3
    bulk_rows = width // pieces

    def bulk_copy(piece, to):
        rows = pl.ds(piece * bulk_rows, bulk_rows)
        return pltpu.make_async_remote_copy(
            src_ref=inner_inv_hbm.at[0, rows],
            dst_ref=root_inv.at[rows],
            send_sem=bulk_send.at[to // 2],
            recv_sem=bulk_recv,
            device_id=(to, m),
            device_id_type=MESH,
        )

    greeted = fronts - 1 + leaves - 1

    @pl.when(is_slot)
    def _():
        pl.semaphore_wait(barrier, greeted)
        slot_map_copy(x + 1).start()

    seed_copy.wait()
    seeds = jnp.zeros((probes, 1), jnp.int32)
    row = lax.broadcasted_iota(jnp.int32, (probes, 1), 0)
    for p in range(probes):
        seeds = jnp.where(row == p, seeds_s[p], seeds)

    piece = 512

    def make_signs(i, carry):
        start = pl.multiple_of(i * piece, piece)
        z = probe_signs(seeds, x, columns, start, (probes, piece))
        signs[:, pl.ds(start, piece)] = z.astype(bf16)
        return carry

    lax.fori_loop(0, columns // piece, make_signs, 0)

    def rows_times(vector, matrix):
        return lax.dot_general(vector, matrix[...], NT, preferred_element_type=f32)

    loads[0].wait()
    leaf_y[...] = rows_times(signs[...], leaf_inv)
    yb_leaf = leaf_y[...].astype(bf16)
    loads[1].wait()
    loads[2].start()
    loads[3].start()
    wide = 2048

    def leaf_products(i, carry):
        at = pl.ds(pl.multiple_of(i * wide, wide), wide)
        leaf_all[:, at] = jnp.dot(
            yb_leaf, leaf_upd[:, at], preferred_element_type=f32
        ).astype(bf16)
        return carry

    lax.fori_loop(0, leaf_upd.shape[1] // wide, leaf_products, 0)
    map_copy.wait()

    @pl.when(jnp.logical_not(is_slot))
    def _():
        pl.semaphore_wait(barrier, greeted)

    @pl.when(is_root)
    def _():
        for to in (0, 2, 3):
            map_to(to, 1).start()
        for q in range(early):
            bulk_copy(q, 0).start()
        for q in range(pieces):
            bulk_copy(q, 2).start()

    blocks = columns // BLOCK
    count = all_maps.shape[2]
    target = lax.broadcasted_iota(jnp.int32, (blocks, count), 0)
    source = lax.broadcasted_iota(jnp.int32, (blocks, count), 1) + 1
    lane = lax.broadcasted_iota(jnp.int32, (blocks, 128), 1)
    sub = lax.broadcasted_iota(jnp.int32, (blocks, 128), 0)

    def find(values, wanted):
        return jnp.max(jnp.where(values == wanted, source, 0), axis=1, keepdims=True)

    def as_row(column):
        return jnp.sum(jnp.where(lane == sub, column, 0), axis=0, keepdims=True)

    def slot_map():
        pair = all_maps[pl.ds((x // 2) * 2, 1)][0]
        return jnp.where(x % 2 == 0, pair[0:1], pair[1:2])

    def table_out(which):
        copy = pltpu.make_async_copy(table_v.at[which], table_s.at[which], small_sem.at[2])
        copy.start()
        copy.wait()

    table_v[...] = jnp.zeros(table_v.shape, jnp.int32)

    @pl.when(jnp.logical_not(is_slot))
    def _():
        slot_map_copy(x).wait_recv()

    table_v[0, 0:1, :] = as_row(find(slot_map(), target))
    table_out(0)

    def pick(read, table, at, rows, write):
        left_half = lax.broadcasted_iota(jnp.int32, (rows, 128), 1) < BLOCK

        def half(entry, side):
            block = jnp.maximum(entry - 1, 0)
            odd = jnp.full((rows, 128), block & 1, jnp.int32)
            found = jnp.full((rows, 128), entry, jnp.int32)
            tile = read((block >> 1) * 128).astype(f32)
            turned = pltpu.roll(tile, BLOCK, 1)
            here = jnp.where(odd == side, tile, turned)
            return jnp.where(found > 0, here, 0.0)

        def body(j, carry):
            first = half(table_s[table, at, 2 * j], 0)
            second = half(table_s[table, at, 2 * j + 1], 1)
            write(j, jnp.where(left_half, first, second).astype(bf16))
            return carry

        lax.fori_loop(0, blocks // 2, body, 0, unroll=4)

    def pick_matrix(matrix, table, at, out):
        def write(j, tile):
            out[:, pl.ds(pl.multiple_of(j * 128, 128), 128)] = tile

        pick(lambda start: matrix[:, pl.ds(start, 128)], table, at, width, write)

    def pick_products(table, at, write):
        pick(lambda start: leaf_all[:, pl.ds(start, 128)], table, at, probes, write)

    def to_peers(src, dst, send_sem, recv_sem):
        def send(i, carry):
            j = peer(i)
            pltpu.make_async_remote_copy(
                src_ref=src(j),
                dst_ref=dst,
                send_sem=send_sem,
                recv_sem=recv_sem,
                device_id=(x, j),
                device_id_type=MESH,
            ).start()
            return carry

        lax.fori_loop(0, fronts - 1, send, 0)

    def wait_for(buffer, sem):
        part = buffer.at[pl.ds(0, fronts - 1)]
        pltpu.make_async_copy(part, part, sem).wait()

    def parts_start(which, h):
        to_peers(
            lambda j: send_part.at[which, h, j],
            recv_part.at[which, h, m],
            part_send.at[which, h],
            part_recv.at[which, h],
        )
        recv_part[which, h, m] = send_part[which, h, m]

    def sum_start(which, h, vector, matrix, more=None):
        partial = jnp.dot(vector, matrix[...], preferred_element_type=f32)
        for j in range(fronts):
            chunk = partial[:, j * width : (j + 1) * width]
            if more is not None:
                chunk = chunk + more[h, j].astype(f32)
            send_part[which, h, j] = chunk.astype(bf16)
        parts_start(which, h)

    def sum_finish(which, h):
        wait_for(recv_part.at[which, h], part_recv.at[which, h])
        sums = []
        for q in range(4):
            total = recv_part[which, h, q].astype(f32)
            for j in range(q + 4, fronts, 4):
                total = total + recv_part[which, h, j].astype(f32)
            sums.append(total)
        return (sums[0] + sums[1]) + (sums[2] + sums[3])

    def share_start(which, h, chunk_ref):
        to_peers(
            lambda j: chunk_ref,
            recv_all.at[which, h, m],
            all_send.at[which, h],
            all_recv.at[which, h],
        )
        recv_all[which, h, m] = chunk_ref[...]

    def share_finish(which, h):
        wait_for(recv_all.at[which, h], all_recv.at[which, h])
        return jnp.concatenate([recv_all[which, h, j] for j in range(fronts)], axis=1)

    def hop(src, dst, send_sem, recv_sem, to):
        return pltpu.make_async_remote_copy(
            src_ref=src,
            dst_ref=dst,
            send_sem=send_sem,
            recv_sem=recv_sem,
            device_id=(to, m),
            device_id_type=MESH,
        )

    LEAF_SUM, ROOT_SUM, ROOT_BACK, SLOT_BACK, LAST_SUM = 0, 1, 2, 3, 4
    SLOT_RHS, ROOT_RHS, ROOT_X, SLOT_X = 0, 1, 2, 3

    def up_copy(h, to):
        return hop(hop_send.at[0, h], hop_up.at[h], hop_up_send.at[h], hop_up_recv.at[h], to)

    def root_copy(h, i, origin, to):
        return hop(
            hop_root.at[origin, h], hop_root.at[origin, h], hop_root_send.at[i, h], hop_root_recv.at[origin, h], to
        )

    def root_x_copy(h, to):
        return hop(hop_send.at[1, h], hop_root_x.at[h], hop_x_send.at[0, h], hop_x_recv.at[0, h], to)

    def slot_x_copy(h, to):
        return hop(own_chunk.at[SLOT_X, h], hop_slot_x.at[h], hop_x_send.at[1, h], hop_x_recv.at[1, h], to)

    def half_of(value, h):
        return value[h * part_rows : (h + 1) * part_rows]

    def write_leaf_part(j, tile):
        for h in halves:
            send_part[LEAF_SUM, h, j] = tile[h * part_rows : (h + 1) * part_rows]

    pick_products(0, 0, write_leaf_part)
    for h in halves:
        parts_start(LEAF_SUM, h)

    @pl.when(jnp.logical_not(is_root))
    def _():
        map_to(0, 1).wait_recv()

    root_pair = all_maps[1]
    root_map = jnp.where(x // 2 == 0, root_pair[0:1], root_pair[1:2])
    inner = find(root_map, target)
    through = find(slot_map(), jnp.where(inner == 0, -1, inner + (blocks - 1)))
    table_v[1, 0:1, :] = as_row(through)
    table_v[1, 1:2, :] = as_row(inner)
    table_out(1)

    @pl.when(jnp.logical_not(is_slot))
    def _():
        for h in halves:
            hop_send[0, h] = sum_finish(LEAF_SUM, h)
            up_copy(h, x - 1).start()

        @pl.when(is_root)
        def _():
            for q in range(early, pieces):
                bulk_copy(q, 0).start()

        def write_root_part(j, tile):
            for h in halves:
                send_part[ROOT_SUM, h, j] = half_of(tile, h)

        pick_products(1, 0, write_root_part)
        for h in halves:
            parts_start(ROOT_SUM, h)
        loads[2].wait()
        loads[3].wait()
        pick_matrix(leaf_upd, 0, 0, to_slot)
        pick_matrix(leaf_upd, 1, 0, to_root)
        for h in halves:
            hop_root[x, h] = sum_finish(ROOT_SUM, h)
            for i, to in enumerate((0, 2)):
                root_copy(h, i, x, to).start()

    @pl.when(is_slot)
    def _():
        def write_carried(j, tile):
            for h in halves:
                carried[h, j] = half_of(tile, h)

        pick_products(1, 0, write_carried)
        loads[2].wait()
        pick_matrix(inner_upd, 1, 1, slot_root)
        slot_signs = probe_signs(seeds, x + 1 + leaves, columns, m * width, (probes, width))
        root_signs = probe_signs(seeds, ROOT_AT + 1 + leaves, columns, m * width, (probes, width))
        loads[3].wait()
        for h in halves:
            own_sum = sum_finish(LEAF_SUM, h)
            up_copy(h, x).wait_recv()
            own_chunk[SLOT_RHS, h] = (half_of(slot_signs, h) - (own_sum + hop_up[h])).astype(bf16)
            share_start(SLOT_RHS, h, own_chunk.at[SLOT_RHS, h])
        pick_matrix(leaf_upd, 0, 0, to_slot)
        for h in halves:
            y_slot = rows_times(share_finish(SLOT_RHS, h), inner_inv)
            inner_y[rows_of(h)] = y_slot
            sum_start(ROOT_SUM, h, y_slot.astype(bf16), slot_root, carried)
        pick_matrix(leaf_upd, 1, 0, to_root)
        for h in halves:
            hop_root[x, h] = sum_finish(ROOT_SUM, h)
            root_copy(h, 0, x, 2 - x).start()
        for h in halves:
            for origin in (1, 3):
                root_copy(h, 0, origin, x).wait_recv()
            root_copy(h, 0, 2 - x, x).wait_recv()
            total = (hop_root[0, h] + hop_root[1, h]) + (hop_root[2, h] + hop_root[3, h])
            own_chunk[ROOT_RHS, h] = (half_of(root_signs, h) - total).astype(bf16)
            share_start(ROOT_RHS, h, own_chunk.at[ROOT_RHS, h])
        pltpu.make_async_copy(root_inv, root_inv, bulk_recv).wait()
        for h in halves:
            y_root = rows_times(share_finish(ROOT_RHS, h), root_inv)
            sum_start(ROOT_BACK, h, y_root.astype(bf16), root_inv)
        for h in halves:
            result = sum_finish(ROOT_BACK, h)
            own_chunk[ROOT_X, h] = result.astype(bf16)
            hop_send[1, h] = result
            root_x_copy(h, x + 1).start()
            share_start(ROOT_X, h, own_chunk.at[ROOT_X, h])
        for h in halves:
            x_root = share_finish(ROOT_X, h)
            s = (inner_y[rows_of(h)] - rows_times(x_root, slot_root)).astype(bf16)
            sum_start(SLOT_BACK, h, s, inner_inv)
        for h in halves:
            x_root = jnp.concatenate([recv_all[ROOT_X, h, j] for j in range(fronts)], axis=1)
            leaf_v[rows_of(h)] = leaf_y[rows_of(h)] - rows_times(x_root, to_root)
        for h in halves:
            result = sum_finish(SLOT_BACK, h)
            own_chunk[SLOT_X, h] = result.astype(bf16)
            slot_x_copy(h, x + 1).start()
            share_start(SLOT_X, h, own_chunk.at[SLOT_X, h])
            inner_out[0, rows_of(h)] = result

    @pl.when(jnp.logical_not(is_slot))
    def _():
        for h in halves:
            root_x_copy(h, x).wait_recv()
            own_chunk[ROOT_X, h] = hop_root_x[h].astype(bf16)
            share_start(ROOT_X, h, own_chunk.at[ROOT_X, h])
            inner_out[0, rows_of(h)] = jnp.where(is_root, hop_root_x[h], 0.0)
        for h in halves:
            x_root = share_finish(ROOT_X, h)
            leaf_v[rows_of(h)] = leaf_y[rows_of(h)] - rows_times(x_root, to_root)
        for h in halves:
            slot_x_copy(h, x).wait_recv()
            share_start(SLOT_X, h, hop_slot_x.at[h])

    for h in halves:
        x_slot = share_finish(SLOT_X, h)
        s = (leaf_v[rows_of(h)] - rows_times(x_slot, to_slot)).astype(bf16)
        sum_start(LAST_SUM, h, s, leaf_inv)
    for h in halves:
        leaf_out[0, rows_of(h)] = sum_finish(LAST_SUM, h)

    for h in halves:
        for which in (LEAF_SUM, ROOT_SUM, LAST_SUM):
            wait_for(send_part.at[which, h], part_send.at[which, h])
        for which in (ROOT_X, SLOT_X):
            wait_for(recv_all.at[which, h], all_send.at[which, h])

    @pl.when(is_slot)
    def _():
        slot_map_copy(x + 1).wait_send()
        for h in halves:
            for which in (ROOT_BACK, SLOT_BACK):
                wait_for(send_part.at[which, h], part_send.at[which, h])
            for which in (SLOT_RHS, ROOT_RHS):
                wait_for(recv_all.at[which, h], all_send.at[which, h])
            root_copy(h, 0, x, 2 - x).wait_send()
            root_x_copy(h, x + 1).wait_send()
            slot_x_copy(h, x + 1).wait_send()

    @pl.when(jnp.logical_not(is_slot))
    def _():
        for h in halves:
            up_copy(h, x - 1).wait_send()
            for i, to in enumerate((0, 2)):
                root_copy(h, i, x, to).wait_send()

    @pl.when(is_root)
    def _():
        for to in (0, 2, 3):
            map_to(to, 1).wait_send()
        for to in (0, 2):
            pltpu.make_async_copy(root_inv, root_inv, bulk_send.at[to // 2]).wait()


def write_out(leaf_ref, inner_ref, leaf_hbm, inner_hbm, sem):
    copies = [
        pltpu.make_async_copy(leaf_ref, leaf_hbm, sem.at[0]),
        pltpu.make_async_copy(inner_ref, inner_hbm, sem.at[1]),
    ]
    for copy in copies:
        copy.start()
    for copy in copies:
        copy.wait()


def shards(probe_seeds, leaf_inverse, leaf_update, internal_inverse, internal_update, child_map):
    fronts = lax.axis_size("front")
    leaves = lax.axis_size("leaf")
    probes = probe_seeds.shape[0]
    width, columns = leaf_inverse.shape[1:]
    rows = leaf_update.shape[2]
    f32, bf16 = jnp.float32, jnp.bfloat16
    dma = pltpu.SemaphoreType.DMA
    vmem = pl.BlockSpec(memory_space=pltpu.VMEM)
    hbm = pl.BlockSpec(memory_space=pltpu.HBM)
    out = jax.ShapeDtypeStruct((1, probes, width), f32)
    part = (probes // 2, width)
    operands = [
        pltpu.with_memory_space_constraint(array, pltpu.HBM)
        for array in (
            probe_seeds, child_map, leaf_inverse, leaf_update, internal_inverse, internal_update,
        )
    ]
    leaf_part, inner_part = pl.pallas_call(
        functools.partial(kernel, fronts, probes, columns, width),
        out_shape=(out, out),
        in_specs=[hbm] * 6,
        out_specs=(vmem, vmem),
        scratch_shapes=[
            pltpu.SMEM((probes,), jnp.int32),
            pltpu.VMEM((width, columns), bf16),
            pltpu.VMEM((width, rows), bf16),
            pltpu.VMEM((width, columns), bf16),
            pltpu.VMEM((width, rows), bf16),
            pltpu.VMEM((width, columns), bf16),
            pltpu.VMEM((width, columns), bf16),
            pltpu.VMEM((width, columns), bf16),
            pltpu.VMEM((width, columns), bf16),
            pltpu.VMEM((probes, columns), bf16),
            pltpu.VMEM((probes, rows), bf16),
            pltpu.VMEM((2, fronts, *part), bf16),
            pltpu.VMEM((leaves, *child_map.shape[1:]), jnp.int32),
            pltpu.VMEM((2, 8, 128), jnp.int32),
            pltpu.SMEM((2, 8, 128), jnp.int32),
            pltpu.VMEM((5, 2, fronts, *part), bf16),
            pltpu.VMEM((5, 2, fronts, *part), bf16),
            pltpu.VMEM((4, 2, *part), bf16),
            pltpu.VMEM((4, 2, fronts, *part), bf16),
            pltpu.VMEM((2, 2, *part), f32),
            pltpu.VMEM((2, *part), f32),
            pltpu.VMEM((leaves, 2, *part), f32),
            pltpu.VMEM((2, *part), f32),
            pltpu.VMEM((2, *part), bf16),
            pltpu.VMEM((probes, width), f32),
            pltpu.VMEM((probes, width), f32),
            pltpu.VMEM((probes, width), f32),
            dma((4,)),
            dma((3,)),
            dma((leaves,)),
            dma((2,)),
            dma((5, 2)),
            dma((5, 2)),
            dma((4, 2)),
            dma((4, 2)),
            dma((2,)),
            dma((2,)),
            dma((2, 2)),
            dma((leaves, 2)),
            dma((2, 2)),
            dma((2, 2)),
            dma((2,)),
            dma,
        ],
        compiler_params=pltpu.CompilerParams(
            collective_id=0, has_side_effects=True, vmem_limit_bytes=48 * 1024 * 1024
        ),
        name="solves",
    )(*operands)
    return pl.pallas_call(
        write_out,
        out_shape=(out, out),
        in_specs=[vmem, vmem],
        out_specs=(hbm, hbm),
        scratch_shapes=[dma((2,))],
        name="write_out",
    )(leaf_part, inner_part)


def solution(mesh):
    return jax.shard_map(
        shards,
        mesh=mesh,
        in_specs=(
            P(),
            P("leaf", "front", None),
            P("leaf", "front", None),
            P("leaf", "front", None),
            P("leaf", "front", None),
            P("leaf", None, None),
        ),
        out_specs=(P("leaf", None, "front"), P("leaf", None, "front")),
        check_vma=False,
    )
```

```python
import functools

import jax
import jax.numpy as jnp
from jax import lax
from jax.experimental import pallas as pl
from jax.experimental.pallas import tpu as pltpu
from jax.sharding import PartitionSpec as P

BLOCK = 64
MOD = 32749
MESH = pl.DeviceIdType.MESH
NT = (((1,), (1,)), ((), ()))
OFFSETS = (
    (2, 2), (2, 1), (1, 2), (2, 3), (3, 2), (2, 0), (0, 2), (1, 1),
    (3, 3), (1, 3), (3, 1), (1, 0), (0, 1), (3, 0), (0, 3), (0, 0),
)


def packed(values):
    word = sum(v << (2 * i) for i, v in enumerate(values))
    return word - (1 << 32) if word >= 1 << 31 else word


OFFSET_Z = packed([z for z, _ in OFFSETS])
OFFSET_Y = packed([y for _, y in OFFSETS])
CHIPS = 16
FAR_CHIPS = 5
FAR = 2 * FAR_CHIPS


def mod_prime(x):
    q = (x.astype(jnp.float32) * (1.0 / MOD)).astype(jnp.int32)
    r = x - q * MOD
    r = jnp.where(r < 0, r + MOD, r)
    return jnp.where(r >= MOD, r - MOD, r)


def probe_signs(seeds, node_id, columns, start, shape):
    index = node_id * columns + start + lax.broadcasted_iota(jnp.int32, shape, 1)
    wrapped = index >= MOD
    lower = jnp.where(wrapped, index - MOD, index)
    upper = jnp.where(wrapped, 1, 0)
    hashed = mod_prime(lower * 30011 + upper * 7717 + seeds)
    hashed = mod_prime(hashed * hashed)
    hashed = mod_prime(hashed * 21143 + lower)
    hashed = mod_prime(hashed * hashed + upper)
    return (1 - 2 * ((hashed >> 3) & 1)).astype(jnp.float32)


def kernel(
    fronts,
    probes,
    columns,
    width,
    seeds_hbm,
    maps_hbm,
    leaf_inv_hbm,
    leaf_upd_hbm,
    inner_inv_hbm,
    inner_upd_hbm,
    leaf_out,
    inner_out,
    seeds_s,
    leaf_inv,
    leaf_upd,
    inner_inv,
    inner_upd,
    to_slot,
    to_root,
    slot_root,
    signs,
    leaf_all,
    carried,
    all_maps,
    table_v,
    table_s,
    send_part,
    recv_part,
    recv_cross,
    own_chunk,
    recv_all,
    hop_send,
    hop_up,
    hop_root,
    leaf_y,
    inner_y,
    leaf_v,
    load_sem,
    small_sem,
    map_send,
    map_recv,
    part_send,
    part_recv,
    cross_send,
    cross_recv,
    all_send,
    all_recv,
    hop_up_send,
    hop_up_recv,
    hop_root_send,
    hop_root_recv,
    hop_x_send,
    hop_x_recv,
):
    x = lax.axis_index("leaf")
    m = lax.axis_index("front")
    m_z, m_y, m_c = m // 8, lax.rem(m // 2, 4), lax.rem(m, 2)
    leaves = 4
    f32, bf16 = jnp.float32, jnp.bfloat16
    is_slot = (x == 0) | (x == 2)
    is_root = x == 1
    part_rows = probes // 2
    halves = (0, 1)

    def rows_of(h):
        return pl.ds(h * part_rows, part_rows)

    seed_copy = pltpu.make_async_copy(seeds_hbm, seeds_s, small_sem.at[0])
    map_copy = pltpu.make_async_copy(maps_hbm.at[0], all_maps.at[x], small_sem.at[1])
    seed_copy.start()
    map_copy.start()
    loads = [
        pltpu.make_async_copy(src.at[0], dst, load_sem.at[i])
        for i, (src, dst) in enumerate(
            (
                (leaf_inv_hbm, leaf_inv),
                (leaf_upd_hbm, leaf_upd),
                (inner_upd_hbm, inner_upd),
                (inner_inv_hbm, inner_inv),
            )
        )
    ]
    loads[0].start()
    loads[1].start()

    def peer(i):
        at = i & 30
        z = (m_z + (jnp.int32(OFFSET_Z) >> at)) & 3
        y = (m_y + (jnp.int32(OFFSET_Y) >> at)) & 3
        return z * 8 + y * 2 + ((m_c + 1 + i) & 1)

    barrier = pltpu.get_barrier_semaphore()

    def greet_front(i, carry):
        pl.semaphore_signal(barrier, inc=1, device_id=(x, peer(i)), device_id_type=MESH)
        return carry

    lax.fori_loop(0, fronts - 1, greet_front, 0)
    for i in range(1, leaves):
        pl.semaphore_signal(
            barrier, inc=1, device_id=(lax.rem(x + i, leaves), m), device_id_type=MESH
        )

    def map_to(to, kind):
        return pltpu.make_async_remote_copy(
            src_ref=maps_hbm.at[0],
            dst_ref=all_maps.at[x],
            send_sem=map_send.at[to],
            recv_sem=map_recv.at[kind],
            device_id=(to, m),
            device_id_type=MESH,
        )

    def slot_map_copy(to):
        return pltpu.make_async_remote_copy(
            src_ref=maps_hbm.at[0],
            dst_ref=all_maps.at[x],
            send_sem=map_send.at[0],
            recv_sem=map_recv.at[0],
            device_id=(to, m),
            device_id_type=MESH,
        )

    greeted = fronts - 1 + leaves - 1

    @pl.when(is_slot)
    def _():
        pl.semaphore_wait(barrier, greeted)
        slot_map_copy(x + 1).start()

    seed_copy.wait()
    seeds = jnp.zeros((probes, 1), jnp.int32)
    row = lax.broadcasted_iota(jnp.int32, (probes, 1), 0)
    for p in range(probes):
        seeds = jnp.where(row == p, seeds_s[p], seeds)

    piece = 512

    def make_signs(i, carry):
        start = pl.multiple_of(i * piece, piece)
        z = probe_signs(seeds, x, columns, start, (probes, piece))
        signs[:, pl.ds(start, piece)] = z.astype(bf16)
        return carry

    lax.fori_loop(0, columns // piece, make_signs, 0)

    def rows_times(vector, matrix):
        return lax.dot_general(vector, matrix[...], NT, preferred_element_type=f32)

    loads[0].wait()
    leaf_y[...] = rows_times(signs[...], leaf_inv)
    yb_leaf = leaf_y[...].astype(bf16)
    loads[1].wait()
    loads[2].start()
    loads[3].start()
    wide = 2048

    def leaf_products(i, carry):
        at = pl.ds(pl.multiple_of(i * wide, wide), wide)
        leaf_all[:, at] = jnp.dot(
            yb_leaf, leaf_upd[:, at], preferred_element_type=f32
        ).astype(bf16)
        return carry

    lax.fori_loop(0, leaf_upd.shape[1] // wide, leaf_products, 0)
    map_copy.wait()

    @pl.when(jnp.logical_not(is_slot))
    def _():
        pl.semaphore_wait(barrier, greeted)

    @pl.when(is_root)
    def _():
        for to in (0, 2, 3):
            map_to(to, 1).start()

    blocks = columns // BLOCK
    count = all_maps.shape[2]
    target = lax.broadcasted_iota(jnp.int32, (blocks, count), 0)
    source = lax.broadcasted_iota(jnp.int32, (blocks, count), 1) + 1
    lane = lax.broadcasted_iota(jnp.int32, (blocks, 128), 1)
    sub = lax.broadcasted_iota(jnp.int32, (blocks, 128), 0)

    def find(values, wanted):
        return jnp.max(jnp.where(values == wanted, source, 0), axis=1, keepdims=True)

    def as_row(column):
        return jnp.sum(jnp.where(lane == sub, column, 0), axis=0, keepdims=True)

    def slot_map():
        pair = all_maps[pl.ds((x // 2) * 2, 1)][0]
        return jnp.where(x % 2 == 0, pair[0:1], pair[1:2])

    def table_out(which):
        copy = pltpu.make_async_copy(table_v.at[which], table_s.at[which], small_sem.at[2])
        copy.start()
        copy.wait()

    table_v[...] = jnp.zeros(table_v.shape, jnp.int32)

    @pl.when(jnp.logical_not(is_slot))
    def _():
        slot_map_copy(x).wait_recv()

    table_v[0, 0:1, :] = as_row(find(slot_map(), target))
    table_out(0)

    def pick(read, table, at, rows, order, write):
        left_half = lax.broadcasted_iota(jnp.int32, (rows, 128), 1) < BLOCK

        def half(entry, side):
            block = jnp.maximum(entry - 1, 0)
            odd = jnp.full((rows, 128), block & 1, jnp.int32)
            found = jnp.full((rows, 128), entry, jnp.int32)
            tile = read((block >> 1) * 128).astype(f32)
            turned = pltpu.roll(tile, BLOCK, 1)
            here = jnp.where(odd == side, tile, turned)
            return jnp.where(found > 0, here, 0.0)

        def body(i, carry):
            j = order(i)
            first = half(table_s[table, at, 2 * j], 0)
            second = half(table_s[table, at, 2 * j + 1], 1)
            write(i, jnp.where(left_half, first, second).astype(bf16))
            return carry

        lax.fori_loop(0, blocks // 2, body, 0, unroll=4)

    def pick_matrix(matrix, table, at, out):
        def write(j, tile):
            out[:, pl.ds(pl.multiple_of(j * 128, 128), 128)] = tile

        pick(lambda start: matrix[:, pl.ds(start, 128)], table, at, width, lambda j: j, write)

    def half_of(value, h):
        return value[h * part_rows : (h + 1) * part_rows]

    def pick_products(table, at, out):
        def write(i, tile):
            for h in halves:
                out[h, i] = half_of(tile, h)

        pick(lambda start: leaf_all[:, pl.ds(start, 128)], table, at, probes, peer, write)

    def send_each(low, high, to, src, dst, send_sem, recv_sem):
        def send(i, carry):
            pltpu.make_async_remote_copy(
                src_ref=src(i),
                dst_ref=dst(i),
                send_sem=send_sem,
                recv_sem=recv_sem,
                device_id=(to, peer(i)),
                device_id_type=MESH,
            ).start()
            return carry

        lax.fori_loop(low, high, send, 0, unroll=2)

    def wait_for(buffer, count, sem):
        part = buffer.at[pl.ds(0, count)]
        pltpu.make_async_copy(part, part, sem).wait()

    NEAR = fronts - 1 - FAR

    def send_far(which, h, cross=None, to=None):
        if cross is None:
            send_each(
                0, FAR, x,
                lambda i: send_part.at[which, h, i],
                lambda i: recv_part.at[which, h, i],
                part_send.at[which, h, 0], part_recv.at[which, h, 0],
            )
        else:
            send_each(
                0, FAR, to,
                lambda i: send_part.at[which, h, i],
                lambda i: recv_cross.at[cross, h, i],
                cross_send.at[0, h], cross_recv.at[cross, h],
            )

    def send_near(which, h):
        send_each(
            FAR, fronts - 1, x,
            lambda i: send_part.at[which, h, i],
            lambda i: recv_part.at[which, h, i],
            part_send.at[which, h, 1], part_recv.at[which, h, 1],
        )
        recv_part[which, h, fronts - 1] = send_part[which, h, fronts - 1]

    def columns_to(t):
        dz, dy = OFFSETS[t]
        chip = ((m_z + dz) & 3) * 4 + ((m_y + dy) & 3)
        return pl.ds(pl.multiple_of(chip * 256, 256), 256)

    def columns_from(t):
        dz, dy = OFFSETS[t]
        chip = ((m_z - dz) & 3) * 4 + ((m_y - dy) & 3)
        return pl.ds(pl.multiple_of(chip * 256, 256), 256)

    def sum_start(which, h, vector, matrix, more=None, cross=None, to=None):
        def chips(low, high):
            for t in range(low, high):
                partial = jnp.dot(vector, matrix[:, columns_to(t)], preferred_element_type=f32)
                for core in (0, 1):
                    i = 2 * t + (m_c if core else 1 - m_c)
                    chunk = partial[:, core * width : (core + 1) * width]
                    if more is not None:
                        chunk = chunk + more[h, i].astype(f32)
                    send_part[which, h, i] = chunk.astype(bf16)

        chips(0, FAR_CHIPS)
        send_far(which, h, cross, to)
        chips(FAR_CHIPS, CHIPS)
        send_near(which, h)

    def add_up(ref, low, high):
        sums = []
        for q in range(low, min(low + 4, high)):
            total = ref[q].astype(f32)
            for j in range(q + 4, high, 4):
                total = total + ref[j].astype(f32)
            sums.append(total)
        return (sums[0] + sums[1]) + (sums[2] + sums[3])

    def near_sum(which, h):
        wait_for(recv_part.at[which, h], NEAR, part_recv.at[which, h, 1])
        return add_up(recv_part.at[which, h], FAR, fronts)

    def sum_finish(which, h):
        total = near_sum(which, h)
        wait_for(recv_part.at[which, h], FAR, part_recv.at[which, h, 0])
        return total + add_up(recv_part.at[which, h], 0, FAR)

    def cross_sum(cross, h):
        wait_for(recv_cross.at[cross, h], FAR, cross_recv.at[cross, h])
        return add_up(recv_cross.at[cross, h], 0, FAR)

    own_at = fronts - 2 + m_c

    def share(which, h, chunk_ref, low, high, to, send_sem):
        send_each(
            low, high, to,
            lambda i: chunk_ref,
            lambda i: recv_all.at[which, h, (i & 30) + m_c],
            send_sem, all_recv.at[which, h, 0 if high == FAR else 1],
        )

    def share_far(which, h, chunk_ref):
        share(which, h, chunk_ref, 0, FAR, x, all_send.at[which, h, 0])

    def share_near(which, h, chunk_ref):
        share(which, h, chunk_ref, FAR, fronts - 1, x, all_send.at[which, h, 1])

    def share_cross(which, h, chunk_ref, to):
        share(which, h, chunk_ref, 0, FAR, to, cross_send.at[1, h])

    def share_all(which, h, chunk_ref):
        share_far(which, h, chunk_ref)
        share_near(which, h, chunk_ref)
        recv_all[which, h, own_at] = chunk_ref[...]

    def shared_times(which, h, matrix, waits=True):
        total = None
        for far, low, high in ((1, FAR_CHIPS, CHIPS), (0, 0, FAR_CHIPS)):
            if waits:
                wait_for(recv_all.at[which, h], NEAR if far else FAR, all_recv.at[which, h, far])
            for t in range(low, high):
                vector = jnp.concatenate(
                    [recv_all[which, h, 2 * t], recv_all[which, h, 2 * t + 1]], axis=1
                )
                term = rows_times(vector, matrix.at[:, columns_from(t)])
                total = term if total is None else total + term
        return total

    def hop(src, dst, send_sem, recv_sem, to):
        return pltpu.make_async_remote_copy(
            src_ref=src,
            dst_ref=dst,
            send_sem=send_sem,
            recv_sem=recv_sem,
            device_id=(to, m),
            device_id_type=MESH,
        )

    LEAF_SUM, ROOT_SUM, BACK_SUM, LAST_SUM = 0, 1, 2, 3
    RESIDUAL, ROOT_X, SLOT_X = 0, 1, 2

    def up_copy(h, to):
        return hop(hop_send.at[h], hop_up.at[h], hop_up_send.at[h], hop_up_recv.at[h], to)

    def root_copy(h, origin):
        return hop(
            hop_root.at[origin, h], hop_root.at[origin, h], hop_root_send.at[h], hop_root_recv.at[origin, h], 1
        )

    def root_x_copy(h, to):
        return hop(
            own_chunk.at[ROOT_X, h], recv_all.at[ROOT_X, h, own_at], hop_x_send.at[to, h], hop_x_recv.at[0, h], to
        )

    def slot_x_copy(h, to):
        return hop(
            own_chunk.at[SLOT_X, h], recv_all.at[SLOT_X, h, own_at], hop_x_send.at[0, h], hop_x_recv.at[1, h], to
        )

    pick_products(0, 0, send_part.at[LEAF_SUM])

    @pl.when(is_slot)
    def _():
        for h in halves:
            send_far(LEAF_SUM, h)
            send_near(LEAF_SUM, h)

    @pl.when(jnp.logical_not(is_slot))
    def _():
        for h in halves:
            send_far(LEAF_SUM, h, 0, x - 1)
            send_near(LEAF_SUM, h)

    @pl.when(jnp.logical_not(is_root))
    def _():
        map_to(0, 1).wait_recv()

    root_pair = all_maps[1]
    root_map = jnp.where(x // 2 == 0, root_pair[0:1], root_pair[1:2])
    inner = find(root_map, target)
    through = find(slot_map(), jnp.where(inner == 0, -1, inner + (blocks - 1)))
    table_v[1, 0:1, :] = as_row(through)
    table_v[1, 1:2, :] = as_row(inner)
    table_out(1)

    @pl.when(jnp.logical_not(is_slot))
    def _():
        for h in halves:
            hop_send[h] = near_sum(LEAF_SUM, h)
            up_copy(h, x - 1).start()
        pick_products(1, 0, send_part.at[ROOT_SUM])
        for h in halves:
            send_far(ROOT_SUM, h)
            send_near(ROOT_SUM, h)
        loads[2].wait()
        loads[3].wait()
        pick_matrix(leaf_upd, 0, 0, to_slot)
        pick_matrix(leaf_upd, 1, 0, to_root)

        @pl.when(x == 3)
        def _():
            for h in halves:
                hop_root[x, h] = sum_finish(ROOT_SUM, h)
                root_copy(h, x).start()

    @pl.when(is_slot)
    def _():
        pick_products(1, 0, carried)
        loads[2].wait()
        pick_matrix(inner_upd, 1, 1, slot_root)
        own_signs = probe_signs(seeds, x + 1 + leaves, columns, m * width, (probes, width))
        loads[3].wait()
        for h in halves:
            own_sum = sum_finish(LEAF_SUM, h)
            own_sum = own_sum + cross_sum(0, h)
            up_copy(h, x).wait_recv()
            own_chunk[RESIDUAL, h] = (half_of(own_signs, h) - (own_sum + hop_up[h])).astype(bf16)
            share_all(RESIDUAL, h, own_chunk.at[RESIDUAL, h])
        pick_matrix(leaf_upd, 0, 0, to_slot)
        for h in halves:
            y_slot = shared_times(RESIDUAL, h, inner_inv)
            inner_y[rows_of(h)] = y_slot
            sum_start(ROOT_SUM, h, y_slot.astype(bf16), slot_root, carried, x // 2, 1)
        pick_matrix(leaf_upd, 1, 0, to_root)
        for h in halves:
            hop_root[x, h] = near_sum(ROOT_SUM, h)
            root_copy(h, x).start()

    @pl.when(is_root)
    def _():
        own_signs = probe_signs(seeds, x + 1 + leaves, columns, m * width, (probes, width))
        for h in halves:
            total = sum_finish(ROOT_SUM, h)
            root_copy(h, 3).wait_recv()
            total = total + hop_root[3, h]
            for i in (0, 1):
                total = total + cross_sum(i, h)
            for i in (0, 1):
                root_copy(h, 2 * i).wait_recv()
                total = total + hop_root[2 * i, h]
            own_chunk[RESIDUAL, h] = (half_of(own_signs, h) - total).astype(bf16)
            share_all(RESIDUAL, h, own_chunk.at[RESIDUAL, h])
        for h in halves:
            y_root = shared_times(RESIDUAL, h, inner_inv)
            sum_start(BACK_SUM, h, y_root.astype(bf16), inner_inv)
        for h in halves:
            result = sum_finish(BACK_SUM, h)
            chunk = own_chunk.at[ROOT_X, h]
            chunk[...] = result.astype(bf16)
            for to in (0, 2):
                root_x_copy(h, to).start()
            for to in (0, 2):
                share_cross(ROOT_X, h, chunk, to)
            root_x_copy(h, 3).start()
            share_all(ROOT_X, h, chunk)
            inner_out[0, rows_of(h)] = result

    @pl.when(is_slot)
    def _():
        for h in halves:
            root_x_copy(h, 0).wait_recv()
            share_near(ROOT_X, h, recv_all.at[ROOT_X, h, own_at])

    @pl.when(x == 3)
    def _():
        for h in halves:
            root_x_copy(h, 0).wait_recv()
            share_far(ROOT_X, h, recv_all.at[ROOT_X, h, own_at])
            share_near(ROOT_X, h, recv_all.at[ROOT_X, h, own_at])
        inner_out[0] = jnp.zeros((probes, width), f32)

    @pl.when(is_slot)
    def _():
        for h in halves:
            v = shared_times(ROOT_X, h, slot_root)
            s = (inner_y[rows_of(h)] - v).astype(bf16)
            sum_start(BACK_SUM, h, s, inner_inv)
        for h in halves:
            leaf_v[rows_of(h)] = leaf_y[rows_of(h)] - shared_times(ROOT_X, h, to_root, False)
        for h in halves:
            result = sum_finish(BACK_SUM, h)
            chunk = own_chunk.at[SLOT_X, h]
            chunk[...] = result.astype(bf16)
            slot_x_copy(h, x + 1).start()
            share_cross(SLOT_X, h, chunk, x + 1)
            share_all(SLOT_X, h, chunk)
            inner_out[0, rows_of(h)] = result

    @pl.when(jnp.logical_not(is_slot))
    def _():
        for h in halves:
            leaf_v[rows_of(h)] = leaf_y[rows_of(h)] - shared_times(ROOT_X, h, to_root)
        for h in halves:
            slot_x_copy(h, x).wait_recv()
            share_near(SLOT_X, h, recv_all.at[SLOT_X, h, own_at])

    for h in halves:
        v = shared_times(SLOT_X, h, to_slot)
        s = (leaf_v[rows_of(h)] - v).astype(bf16)
        sum_start(LAST_SUM, h, s, leaf_inv)
    for h in halves:
        leaf_out[0, rows_of(h)] = sum_finish(LAST_SUM, h)

    def far_left(buffer, sem):
        wait_for(buffer, FAR, sem)

    def near_left(buffer, sem):
        wait_for(buffer, NEAR, sem)

    for h in halves:
        for which in (LEAF_SUM, ROOT_SUM, LAST_SUM):
            near_left(send_part.at[which, h], part_send.at[which, h, 1])
        far_left(send_part.at[LAST_SUM, h], part_send.at[LAST_SUM, h, 0])
        far_left(send_part.at[LEAF_SUM, h], cross_send.at[0, h])
        for which in (ROOT_X, SLOT_X):
            near_left(recv_all.at[which, h], all_send.at[which, h, 1])

    @pl.when(x != 3)
    def _():
        for h in halves:
            far_left(send_part.at[BACK_SUM, h], part_send.at[BACK_SUM, h, 0])
            near_left(send_part.at[BACK_SUM, h], part_send.at[BACK_SUM, h, 1])
            far_left(recv_all.at[RESIDUAL, h], all_send.at[RESIDUAL, h, 0])
            near_left(recv_all.at[RESIDUAL, h], all_send.at[RESIDUAL, h, 1])

    @pl.when(is_slot)
    def _():
        slot_map_copy(x + 1).wait_send()
        for h in halves:
            far_left(send_part.at[LEAF_SUM, h], part_send.at[LEAF_SUM, h, 0])
            root_copy(h, x).wait_send()
            far_left(recv_all.at[SLOT_X, h], all_send.at[SLOT_X, h, 0])
            far_left(recv_all.at[SLOT_X, h], cross_send.at[1, h])
            slot_x_copy(h, x + 1).wait_send()

    @pl.when(jnp.logical_not(is_slot))
    def _():
        for h in halves:
            up_copy(h, x - 1).wait_send()
            far_left(send_part.at[ROOT_SUM, h], part_send.at[ROOT_SUM, h, 0])
            far_left(recv_all.at[ROOT_X, h], all_send.at[ROOT_X, h, 0])

    @pl.when(x == 3)
    def _():
        for h in halves:
            root_copy(h, x).wait_send()

    @pl.when(is_root)
    def _():
        for to in (0, 2, 3):
            map_to(to, 1).wait_send()
        for h in halves:
            wait_for(recv_all.at[ROOT_X, h], 2 * FAR, cross_send.at[1, h])
            for to in (0, 2, 3):
                root_x_copy(h, to).wait_send()


def shards(probe_seeds, leaf_inverse, leaf_update, internal_inverse, internal_update, child_map):
    fronts = lax.axis_size("front")
    leaves = lax.axis_size("leaf")
    probes = probe_seeds.shape[0]
    width, columns = leaf_inverse.shape[1:]
    rows = leaf_update.shape[2]
    f32, bf16 = jnp.float32, jnp.bfloat16
    dma = pltpu.SemaphoreType.DMA
    vmem = pl.BlockSpec(memory_space=pltpu.VMEM)
    hbm = pl.BlockSpec(memory_space=pltpu.HBM)
    out = jax.ShapeDtypeStruct((1, probes, width), f32)
    part = (probes // 2, width)
    operands = [
        pltpu.with_memory_space_constraint(array, pltpu.HBM)
        for array in (
            probe_seeds, child_map, leaf_inverse, leaf_update, internal_inverse, internal_update,
        )
    ]
    return pl.pallas_call(
        functools.partial(kernel, fronts, probes, columns, width),
        out_shape=(out, out),
        in_specs=[hbm] * 6,
        out_specs=(vmem, vmem),
        scratch_shapes=[
            pltpu.SMEM((probes,), jnp.int32),
            pltpu.VMEM((width, columns), bf16),
            pltpu.VMEM((width, rows), bf16),
            pltpu.VMEM((width, columns), bf16),
            pltpu.VMEM((width, rows), bf16),
            pltpu.VMEM((width, columns), bf16),
            pltpu.VMEM((width, columns), bf16),
            pltpu.VMEM((width, columns), bf16),
            pltpu.VMEM((probes, columns), bf16),
            pltpu.VMEM((probes, rows), bf16),
            pltpu.VMEM((2, fronts, *part), bf16),
            pltpu.VMEM((leaves, *child_map.shape[1:]), jnp.int32),
            pltpu.VMEM((2, 8, 128), jnp.int32),
            pltpu.SMEM((2, 8, 128), jnp.int32),
            pltpu.VMEM((4, 2, fronts, *part), bf16),
            pltpu.VMEM((4, 2, fronts, *part), bf16),
            pltpu.VMEM((2, 2, FAR, *part), bf16),
            pltpu.VMEM((3, 2, *part), bf16),
            pltpu.VMEM((3, 2, fronts, *part), bf16),
            pltpu.VMEM((2, *part), f32),
            pltpu.VMEM((2, *part), f32),
            pltpu.VMEM((leaves, 2, *part), f32),
            pltpu.VMEM((probes, width), f32),
            pltpu.VMEM((probes, width), f32),
            pltpu.VMEM((probes, width), f32),
            dma((4,)),
            dma((3,)),
            dma((leaves,)),
            dma((2,)),
            dma((4, 2, 2)),
            dma((4, 2, 2)),
            dma((2, 2)),
            dma((2, 2)),
            dma((3, 2, 2)),
            dma((3, 2, 2)),
            dma((2,)),
            dma((2,)),
            dma((2,)),
            dma((leaves, 2)),
            dma((leaves, 2)),
            dma((2, 2)),
        ],
        compiler_params=pltpu.CompilerParams(
            collective_id=0, has_side_effects=True, vmem_limit_bytes=48 * 1024 * 1024
        ),
        name="solves",
    )(*operands)


def solution(mesh):
    return jax.shard_map(
        shards,
        mesh=mesh,
        in_specs=(
            P(),
            P("leaf", "front", None),
            P("leaf", "front", None),
            P("leaf", "front", None),
            P("leaf", "front", None),
            P("leaf", None, None),
        ),
        out_specs=(P("leaf", None, "front"), P("leaf", None, "front")),
        check_vma=False,
    )
```

```python
import functools

import jax
import jax.numpy as jnp
from jax import lax
from jax.experimental import pallas as pl
from jax.experimental.pallas import tpu as pltpu
from jax.sharding import PartitionSpec as P

BLOCK = 64
MOD = 32749
MESH = pl.DeviceIdType.MESH
NT = (((1,), (1,)), ((), ()))
OFFSETS = (
    (2, 2), (2, 1), (1, 2), (2, 3), (3, 2), (2, 0), (0, 2), (1, 1),
    (3, 3), (1, 3), (3, 1), (1, 0), (0, 1), (3, 0), (0, 3), (0, 0),
)


def packed(values):
    word = sum(v << (2 * i) for i, v in enumerate(values))
    return word - (1 << 32) if word >= 1 << 31 else word


OFFSET_Z = packed([z for z, _ in OFFSETS])
OFFSET_Y = packed([y for _, y in OFFSETS])
CHIPS = 16
FAR_CHIPS = 5
FAR = 2 * FAR_CHIPS
TO_FIRST = (4, 8)
TO_SECOND = 12


def mod_prime(x):
    q = (x.astype(jnp.float32) * (1.0 / MOD)).astype(jnp.int32)
    r = x - q * MOD
    r = jnp.where(r < 0, r + MOD, r)
    return jnp.where(r >= MOD, r - MOD, r)


def probe_signs(seeds, node_id, columns, start, shape):
    index = node_id * columns + start + lax.broadcasted_iota(jnp.int32, shape, 1)
    wrapped = index >= MOD
    lower = jnp.where(wrapped, index - MOD, index)
    upper = jnp.where(wrapped, 1, 0)
    hashed = mod_prime(lower * 30011 + upper * 7717 + seeds)
    hashed = mod_prime(hashed * hashed)
    hashed = mod_prime(hashed * 21143 + lower)
    hashed = mod_prime(hashed * hashed + upper)
    return (1 - 2 * ((hashed >> 3) & 1)).astype(jnp.float32)


def kernel(
    fronts,
    probes,
    columns,
    width,
    seeds_hbm,
    maps_hbm,
    leaf_inv_hbm,
    leaf_upd_hbm,
    inner_inv_hbm,
    inner_upd_hbm,
    leaf_out,
    inner_out,
    seeds_s,
    leaf_inv,
    leaf_upd,
    inner_inv,
    inner_upd,
    to_slot,
    to_root,
    slot_root,
    root_inv,
    signs,
    leaf_all,
    carried,
    all_maps,
    table_v,
    table_in,
    table_s,
    send_part,
    recv_part,
    recv_cross,
    own_chunk,
    recv_all,
    hop_send,
    hop_up,
    hop_root,
    hop_root_x,
    leaf_y,
    inner_y,
    leaf_v,
    load_sem,
    small_sem,
    map_send,
    map_recv,
    part_send,
    part_recv,
    cross_send,
    cross_recv,
    all_send,
    all_recv,
    hop_up_send,
    hop_up_recv,
    hop_root_send,
    hop_root_recv,
    hop_x_send,
    hop_x_recv,
    bulk_send,
    bulk_recv,
):
    x = lax.axis_index("leaf")
    m = lax.axis_index("front")
    m_z, m_y, m_c = m // 8, lax.rem(m // 2, 4), lax.rem(m, 2)
    leaves = 4
    f32, bf16 = jnp.float32, jnp.bfloat16
    is_slot = (x == 0) | (x == 2)
    is_root = x == 1
    part_rows = probes // 2
    halves = (0, 1)

    def rows_of(h):
        return pl.ds(h * part_rows, part_rows)

    seed_copy = pltpu.make_async_copy(seeds_hbm, seeds_s, small_sem.at[0])
    map_copy = pltpu.make_async_copy(maps_hbm.at[0], all_maps.at[x], small_sem.at[1])
    seed_copy.start()
    map_copy.start()
    loads = [
        pltpu.make_async_copy(src.at[0], dst, load_sem.at[i])
        for i, (src, dst) in enumerate(
            (
                (leaf_inv_hbm, leaf_inv),
                (leaf_upd_hbm, leaf_upd),
                (inner_upd_hbm, inner_upd),
                (inner_inv_hbm, inner_inv),
            )
        )
    ]
    loads[0].start()
    loads[1].start()

    def peer(i):
        at = i & 30
        z = (m_z + (jnp.int32(OFFSET_Z) >> at)) & 3
        y = (m_y + (jnp.int32(OFFSET_Y) >> at)) & 3
        return z * 8 + y * 2 + ((m_c + 1 + i) & 1)

    barrier = pltpu.get_barrier_semaphore()

    def greet_front(i, carry):
        pl.semaphore_signal(barrier, inc=1, device_id=(x, peer(i)), device_id_type=MESH)
        return carry

    lax.fori_loop(0, fronts - 1, greet_front, 0)
    for i in range(1, leaves):
        pl.semaphore_signal(
            barrier, inc=1, device_id=(lax.rem(x + i, leaves), m), device_id_type=MESH
        )

    def map_to(to, kind):
        return pltpu.make_async_remote_copy(
            src_ref=maps_hbm.at[0],
            dst_ref=all_maps.at[x],
            send_sem=map_send.at[to],
            recv_sem=map_recv.at[kind],
            device_id=(to, m),
            device_id_type=MESH,
        )

    def slot_map_copy(to):
        return pltpu.make_async_remote_copy(
            src_ref=maps_hbm.at[0],
            dst_ref=all_maps.at[x],
            send_sem=map_send.at[0],
            recv_sem=map_recv.at[0],
            device_id=(to, m),
            device_id_type=MESH,
        )

    pieces = 16
    bulk_rows = width // pieces

    def bulk_copy(piece, to):
        rows = pl.ds(piece * bulk_rows, bulk_rows)
        return pltpu.make_async_remote_copy(
            src_ref=inner_inv_hbm.at[0, rows],
            dst_ref=root_inv.at[rows],
            send_sem=bulk_send.at[to // 2],
            recv_sem=bulk_recv,
            device_id=(to, m),
            device_id_type=MESH,
        )

    greeted = fronts - 1 + leaves - 1

    seed_copy.wait()
    seeds = jnp.zeros((probes, 1), jnp.int32)
    row = lax.broadcasted_iota(jnp.int32, (probes, 1), 0)
    for p in range(probes):
        seeds = jnp.where(row == p, seeds_s[p], seeds)

    piece = 512

    def make_signs(i, carry):
        start = pl.multiple_of(i * piece, piece)
        z = probe_signs(seeds, x, columns, start, (probes, piece))
        signs[:, pl.ds(start, piece)] = z.astype(bf16)
        return carry

    lax.fori_loop(0, columns // piece, make_signs, 0)

    def rows_times(vector, matrix):
        return lax.dot_general(vector, matrix[...], NT, preferred_element_type=f32)

    loads[0].wait()
    leaf_y[...] = rows_times(signs[...], leaf_inv)
    yb_leaf = leaf_y[...].astype(bf16)
    loads[1].wait()
    loads[2].start()
    loads[3].start()
    blocks = columns // BLOCK
    count = all_maps.shape[2]
    target = lax.broadcasted_iota(jnp.int32, (blocks, count), 0)
    source = lax.broadcasted_iota(jnp.int32, (blocks, count), 1) + 1
    lane = lax.broadcasted_iota(jnp.int32, (blocks, 128), 1)
    sub = lax.broadcasted_iota(jnp.int32, (blocks, 128), 0)

    def find(values, wanted):
        return jnp.max(jnp.where(values == wanted, source, 0), axis=1, keepdims=True)

    def as_row(column):
        return jnp.sum(jnp.where(lane == sub, column, 0), axis=0, keepdims=True)

    def slot_map():
        pair = all_maps[pl.ds((x // 2) * 2, 1)][0]
        return jnp.where(x % 2 == 0, pair[0:1], pair[1:2])

    def table_out(which):
        copy = pltpu.make_async_copy(table_v.at[which], table_s.at[which], small_sem.at[2])
        copy.start()
        copy.wait()

    table_v[...] = jnp.zeros(table_v.shape, jnp.int32)

    def child_table_copy(to):
        return pltpu.make_async_remote_copy(
            src_ref=table_v.at[2],
            dst_ref=table_in,
            send_sem=map_send.at[1],
            recv_sem=map_recv.at[2],
            device_id=(to, m),
            device_id_type=MESH,
        )

    @pl.when(is_slot)
    def _():
        map_copy.wait()
        pair = all_maps[pl.ds(x, 1)][0]
        table_v[0, 0:1, :] = as_row(find(pair[0:1], target))
        table_v[2, 0:1, :] = as_row(find(pair[1:2], target))
        pl.semaphore_wait(barrier, greeted)
        child_table_copy(x + 1).start()
        slot_map_copy(x + 1).start()
        table_out(0)

    wide = 2048

    def leaf_products(i, carry):
        at = pl.ds(pl.multiple_of(i * wide, wide), wide)
        leaf_all[:, at] = jnp.dot(
            yb_leaf, leaf_upd[:, at], preferred_element_type=f32
        ).astype(bf16)
        return carry

    lax.fori_loop(0, leaf_upd.shape[1] // wide, leaf_products, 0)
    @pl.when(jnp.logical_not(is_slot))
    def _():
        map_copy.wait()
        pl.semaphore_wait(barrier, greeted)

    @pl.when(is_root)
    def _():
        for to in (0, 2, 3):
            map_to(to, 1).start()
        for q in range(TO_FIRST[0]):
            bulk_copy(q, 0).start()
        for q in range(TO_SECOND):
            bulk_copy(q, 2).start()

    def pick(read, table, at, rows, order, write):
        left_half = lax.broadcasted_iota(jnp.int32, (rows, 128), 1) < BLOCK

        def half(entry, side):
            block = jnp.maximum(entry - 1, 0)
            odd = jnp.full((rows, 128), block & 1, jnp.int32)
            found = jnp.full((rows, 128), entry, jnp.int32)
            tile = read((block >> 1) * 128).astype(f32)
            turned = pltpu.roll(tile, BLOCK, 1)
            here = jnp.where(odd == side, tile, turned)
            return jnp.where(found > 0, here, 0.0)

        def body(i, carry):
            j = order(i)
            first = half(table_s[table, at, 2 * j], 0)
            second = half(table_s[table, at, 2 * j + 1], 1)
            write(i, jnp.where(left_half, first, second).astype(bf16))
            return carry

        lax.fori_loop(0, blocks // 2, body, 0, unroll=4)

    def pick_matrix(matrix, table, at, out):
        def write(j, tile):
            out[:, pl.ds(pl.multiple_of(j * 128, 128), 128)] = tile

        pick(lambda start: matrix[:, pl.ds(start, 128)], table, at, width, lambda j: j, write)

    def half_of(value, h):
        return value[h * part_rows : (h + 1) * part_rows]

    def pick_products(table, at, out):
        def write(i, tile):
            for h in halves:
                out[h, i] = half_of(tile, h)

        pick(lambda start: leaf_all[:, pl.ds(start, 128)], table, at, probes, peer, write)

    def send_each(low, high, to, src, dst, send_sem, recv_sem):
        def send(i, carry):
            pltpu.make_async_remote_copy(
                src_ref=src(i),
                dst_ref=dst(i),
                send_sem=send_sem,
                recv_sem=recv_sem,
                device_id=(to, peer(i)),
                device_id_type=MESH,
            ).start()
            return carry

        lax.fori_loop(low, high, send, 0, unroll=2)

    def wait_for(buffer, count, sem):
        part = buffer.at[pl.ds(0, count)]
        pltpu.make_async_copy(part, part, sem).wait()

    NEAR = fronts - 1 - FAR

    def send_far(which, h, to=None):
        if to is None:
            send_each(
                0, FAR, x,
                lambda i: send_part.at[which, h, i],
                lambda i: recv_part.at[which, h, i],
                part_send.at[which, h, 0], part_recv.at[which, h, 0],
            )
        else:
            send_each(
                0, FAR, to,
                lambda i: send_part.at[which, h, i],
                lambda i: recv_cross.at[h, i],
                cross_send.at[0, h], cross_recv.at[h],
            )

    def send_near(which, h):
        send_each(
            FAR, fronts - 1, x,
            lambda i: send_part.at[which, h, i],
            lambda i: recv_part.at[which, h, i],
            part_send.at[which, h, 1], part_recv.at[which, h, 1],
        )
        recv_part[which, h, fronts - 1] = send_part[which, h, fronts - 1]

    def columns_to(t):
        dz, dy = OFFSETS[t]
        chip = ((m_z + dz) & 3) * 4 + ((m_y + dy) & 3)
        return pl.ds(pl.multiple_of(chip * 256, 256), 256)

    def columns_from(t):
        dz, dy = OFFSETS[t]
        chip = ((m_z - dz) & 3) * 4 + ((m_y - dy) & 3)
        return pl.ds(pl.multiple_of(chip * 256, 256), 256)

    def sum_start(which, h, vector, matrix, more=None):
        def chips(low, high):
            for t in range(low, high):
                partial = jnp.dot(vector, matrix[:, columns_to(t)], preferred_element_type=f32)
                for core in (0, 1):
                    i = 2 * t + (m_c if core else 1 - m_c)
                    chunk = partial[:, core * width : (core + 1) * width]
                    if more is not None:
                        chunk = chunk + more[h, i].astype(f32)
                    send_part[which, h, i] = chunk.astype(bf16)

        chips(0, FAR_CHIPS)
        send_far(which, h)
        chips(FAR_CHIPS, CHIPS)
        send_near(which, h)

    def add_up(ref, low, high):
        sums = []
        for q in range(low, min(low + 4, high)):
            total = ref[q].astype(f32)
            for j in range(q + 4, high, 4):
                total = total + ref[j].astype(f32)
            sums.append(total)
        return (sums[0] + sums[1]) + (sums[2] + sums[3])

    def near_sum(which, h):
        wait_for(recv_part.at[which, h], NEAR, part_recv.at[which, h, 1])
        return add_up(recv_part.at[which, h], FAR, fronts)

    def sum_finish(which, h):
        total = near_sum(which, h)
        wait_for(recv_part.at[which, h], FAR, part_recv.at[which, h, 0])
        return total + add_up(recv_part.at[which, h], 0, FAR)

    def cross_sum(h):
        wait_for(recv_cross.at[h], FAR, cross_recv.at[h])
        return add_up(recv_cross.at[h], 0, FAR)

    own_at = fronts - 2 + m_c

    def share(which, h, chunk_ref, low, high, to, send_sem):
        send_each(
            low, high, to,
            lambda i: chunk_ref,
            lambda i: recv_all.at[which, h, (i & 30) + m_c],
            send_sem, all_recv.at[which, h, 0 if high == FAR else 1],
        )

    def share_far(which, h, chunk_ref):
        share(which, h, chunk_ref, 0, FAR, x, all_send.at[which, h, 0])

    def share_near(which, h, chunk_ref):
        share(which, h, chunk_ref, FAR, fronts - 1, x, all_send.at[which, h, 1])

    def share_cross(which, h, chunk_ref, to):
        share(which, h, chunk_ref, 0, FAR, to, cross_send.at[1, h])

    def share_all(which, h, chunk_ref):
        share_far(which, h, chunk_ref)
        share_near(which, h, chunk_ref)
        recv_all[which, h, own_at] = chunk_ref[...]

    def shared_times(which, h, matrix, waits=True):
        total = None
        for far, low, high in ((1, FAR_CHIPS, CHIPS), (0, 0, FAR_CHIPS)):
            if waits:
                wait_for(recv_all.at[which, h], NEAR if far else FAR, all_recv.at[which, h, far])
            for t in range(low, high):
                vector = jnp.concatenate(
                    [recv_all[which, h, 2 * t], recv_all[which, h, 2 * t + 1]], axis=1
                )
                term = rows_times(vector, matrix.at[:, columns_from(t)])
                total = term if total is None else total + term
        return total

    def hop(src, dst, send_sem, recv_sem, to):
        return pltpu.make_async_remote_copy(
            src_ref=src,
            dst_ref=dst,
            send_sem=send_sem,
            recv_sem=recv_sem,
            device_id=(to, m),
            device_id_type=MESH,
        )

    LEAF_SUM, ROOT_SUM, ROOT_BACK, SLOT_BACK, LAST_SUM = 0, 1, 2, 3, 4
    SLOT_RHS, ROOT_RHS, ROOT_X, SLOT_X = 0, 1, 2, 3

    def up_copy(h, to):
        return hop(hop_send.at[0, h], hop_up.at[h], hop_up_send.at[h], hop_up_recv.at[h], to)

    def root_copy(h, i, origin, to):
        return hop(
            hop_root.at[origin, h], hop_root.at[origin, h], hop_root_send.at[i, h], hop_root_recv.at[origin, h], to
        )

    def root_x_copy(h, to):
        return hop(hop_send.at[1, h], hop_root_x.at[h], hop_x_send.at[1, h], hop_x_recv.at[0, h], to)

    def slot_x_copy(h, to):
        return hop(
            own_chunk.at[SLOT_X, h], recv_all.at[SLOT_X, h, own_at], hop_x_send.at[0, h], hop_x_recv.at[1, h], to
        )

    @pl.when(jnp.logical_not(is_slot))
    def _():
        child_table_copy(x).wait_recv()
        arrived = pltpu.make_async_copy(table_in, table_s.at[0], small_sem.at[2])
        arrived.start()
        arrived.wait()

    pick_products(0, 0, send_part.at[LEAF_SUM])

    @pl.when(is_slot)
    def _():
        for h in halves:
            send_far(LEAF_SUM, h)
            send_near(LEAF_SUM, h)

    @pl.when(jnp.logical_not(is_slot))
    def _():
        for h in halves:
            send_far(LEAF_SUM, h, x - 1)
            send_near(LEAF_SUM, h)

    @pl.when(jnp.logical_not(is_root))
    def _():
        map_to(0, 1).wait_recv()

    @pl.when(jnp.logical_not(is_slot))
    def _():
        slot_map_copy(x).wait_recv()

    root_pair = all_maps[1]
    root_map = jnp.where(x // 2 == 0, root_pair[0:1], root_pair[1:2])
    inner = find(root_map, target)
    through = find(slot_map(), jnp.where(inner == 0, -1, inner + (blocks - 1)))
    table_v[1, 0:1, :] = as_row(through)
    table_v[1, 1:2, :] = as_row(inner)
    table_out(1)

    @pl.when(jnp.logical_not(is_slot))
    def _():
        for h in halves:
            hop_send[0, h] = near_sum(LEAF_SUM, h)
            up_copy(h, x - 1).start()

        @pl.when(is_root)
        def _():
            for q in range(*TO_FIRST):
                bulk_copy(q, 0).start()

        pick_products(1, 0, send_part.at[ROOT_SUM])
        for h in halves:
            send_far(ROOT_SUM, h)
            send_near(ROOT_SUM, h)
        loads[2].wait()
        loads[3].wait()
        pick_matrix(leaf_upd, 0, 0, to_slot)
        pick_matrix(leaf_upd, 1, 0, to_root)
        for h in halves:
            hop_root[x, h] = sum_finish(ROOT_SUM, h)
            for i, to in enumerate((0, 2)):
                root_copy(h, i, x, to).start()

        @pl.when(is_root)
        def _():
            for q in range(TO_FIRST[1], pieces):
                bulk_copy(q, 0).start()
            for q in range(TO_SECOND, pieces):
                bulk_copy(q, 2).start()

    @pl.when(is_slot)
    def _():
        pick_products(1, 0, carried)
        loads[2].wait()
        pick_matrix(inner_upd, 1, 1, slot_root)
        slot_signs = probe_signs(seeds, x + 1 + leaves, columns, m * width, (probes, width))
        root_signs = probe_signs(seeds, 2 + leaves, columns, m * width, (probes, width))
        loads[3].wait()
        for h in halves:
            own_sum = sum_finish(LEAF_SUM, h)
            own_sum = own_sum + cross_sum(h)
            up_copy(h, x).wait_recv()
            own_chunk[SLOT_RHS, h] = (half_of(slot_signs, h) - (own_sum + hop_up[h])).astype(bf16)
            share_all(SLOT_RHS, h, own_chunk.at[SLOT_RHS, h])
        pick_matrix(leaf_upd, 0, 0, to_slot)
        for h in halves:
            y_slot = shared_times(SLOT_RHS, h, inner_inv)
            inner_y[rows_of(h)] = y_slot
            sum_start(ROOT_SUM, h, y_slot.astype(bf16), slot_root, carried)
        pick_matrix(leaf_upd, 1, 0, to_root)
        for h in halves:
            hop_root[x, h] = sum_finish(ROOT_SUM, h)
            root_copy(h, 0, x, 2 - x).start()
        for h in halves:
            for origin in (1, 3):
                root_copy(h, 0, origin, x).wait_recv()
            root_copy(h, 0, 2 - x, x).wait_recv()
            total = (hop_root[0, h] + hop_root[1, h]) + (hop_root[2, h] + hop_root[3, h])
            own_chunk[ROOT_RHS, h] = (half_of(root_signs, h) - total).astype(bf16)
            share_all(ROOT_RHS, h, own_chunk.at[ROOT_RHS, h])
        pltpu.make_async_copy(root_inv, root_inv, bulk_recv).wait()
        for h in halves:
            y_root = shared_times(ROOT_RHS, h, root_inv)
            sum_start(ROOT_BACK, h, y_root.astype(bf16), root_inv)
        for h in halves:
            result = sum_finish(ROOT_BACK, h)
            own_chunk[ROOT_X, h] = result.astype(bf16)
            share_all(ROOT_X, h, own_chunk.at[ROOT_X, h])
            hop_send[1, h] = result
            root_x_copy(h, x + 1).start()
        for h in halves:
            v = shared_times(ROOT_X, h, slot_root)
            s = (inner_y[rows_of(h)] - v).astype(bf16)
            sum_start(SLOT_BACK, h, s, inner_inv)
        for h in halves:
            leaf_v[rows_of(h)] = leaf_y[rows_of(h)] - shared_times(ROOT_X, h, to_root, False)
        for h in halves:
            result = sum_finish(SLOT_BACK, h)
            chunk = own_chunk.at[SLOT_X, h]
            chunk[...] = result.astype(bf16)
            slot_x_copy(h, x + 1).start()
            share_cross(SLOT_X, h, chunk, x + 1)
            share_all(SLOT_X, h, chunk)
            inner_out[0, rows_of(h)] = result

    @pl.when(jnp.logical_not(is_slot))
    def _():
        for h in halves:
            root_x_copy(h, x).wait_recv()
            own_chunk[ROOT_X, h] = hop_root_x[h].astype(bf16)
            share_all(ROOT_X, h, own_chunk.at[ROOT_X, h])
            inner_out[0, rows_of(h)] = jnp.where(is_root, hop_root_x[h], 0.0)
        for h in halves:
            leaf_v[rows_of(h)] = leaf_y[rows_of(h)] - shared_times(ROOT_X, h, to_root)
        for h in halves:
            slot_x_copy(h, x).wait_recv()
            share_near(SLOT_X, h, recv_all.at[SLOT_X, h, own_at])

    for h in halves:
        v = shared_times(SLOT_X, h, to_slot)
        s = (leaf_v[rows_of(h)] - v).astype(bf16)
        sum_start(LAST_SUM, h, s, leaf_inv)
    for h in halves:
        leaf_out[0, rows_of(h)] = sum_finish(LAST_SUM, h)

    def far_left(buffer, sem):
        wait_for(buffer, FAR, sem)

    def near_left(buffer, sem):
        wait_for(buffer, NEAR, sem)

    for h in halves:
        for which in (LEAF_SUM, ROOT_SUM, LAST_SUM):
            near_left(send_part.at[which, h], part_send.at[which, h, 1])
        for which in (ROOT_SUM, LAST_SUM):
            far_left(send_part.at[which, h], part_send.at[which, h, 0])
        far_left(recv_all.at[ROOT_X, h], all_send.at[ROOT_X, h, 0])
        for which in (ROOT_X, SLOT_X):
            near_left(recv_all.at[which, h], all_send.at[which, h, 1])

    @pl.when(is_slot)
    def _():
        slot_map_copy(x + 1).wait_send()
        child_table_copy(x + 1).wait_send()
        for h in halves:
            far_left(send_part.at[LEAF_SUM, h], part_send.at[LEAF_SUM, h, 0])
            for which in (ROOT_BACK, SLOT_BACK):
                far_left(send_part.at[which, h], part_send.at[which, h, 0])
                near_left(send_part.at[which, h], part_send.at[which, h, 1])
            for which in (SLOT_RHS, ROOT_RHS):
                far_left(recv_all.at[which, h], all_send.at[which, h, 0])
                near_left(recv_all.at[which, h], all_send.at[which, h, 1])
            root_copy(h, 0, x, 2 - x).wait_send()
            root_x_copy(h, x + 1).wait_send()
            far_left(recv_all.at[SLOT_X, h], all_send.at[SLOT_X, h, 0])
            far_left(recv_all.at[SLOT_X, h], cross_send.at[1, h])
            slot_x_copy(h, x + 1).wait_send()

    @pl.when(jnp.logical_not(is_slot))
    def _():
        for h in halves:
            far_left(send_part.at[LEAF_SUM, h], cross_send.at[0, h])
            up_copy(h, x - 1).wait_send()
            for i, to in enumerate((0, 2)):
                root_copy(h, i, x, to).wait_send()

    @pl.when(is_root)
    def _():
        for to in (0, 2, 3):
            map_to(to, 1).wait_send()
        for to in (0, 2):
            pltpu.make_async_copy(root_inv, root_inv, bulk_send.at[to // 2]).wait()


def shards(probe_seeds, leaf_inverse, leaf_update, internal_inverse, internal_update, child_map):
    fronts = lax.axis_size("front")
    leaves = lax.axis_size("leaf")
    probes = probe_seeds.shape[0]
    width, columns = leaf_inverse.shape[1:]
    rows = leaf_update.shape[2]
    f32, bf16 = jnp.float32, jnp.bfloat16
    dma = pltpu.SemaphoreType.DMA
    vmem = pl.BlockSpec(memory_space=pltpu.VMEM)
    hbm = pl.BlockSpec(memory_space=pltpu.HBM)
    out = jax.ShapeDtypeStruct((1, probes, width), f32)
    part = (probes // 2, width)
    operands = [
        pltpu.with_memory_space_constraint(array, pltpu.HBM)
        for array in (
            probe_seeds, child_map, leaf_inverse, leaf_update, internal_inverse, internal_update,
        )
    ]
    return pl.pallas_call(
        functools.partial(kernel, fronts, probes, columns, width),
        out_shape=(out, out),
        in_specs=[hbm] * 6,
        out_specs=(vmem, vmem),
        scratch_shapes=[
            pltpu.SMEM((probes,), jnp.int32),
            pltpu.VMEM((width, columns), bf16),
            pltpu.VMEM((width, rows), bf16),
            pltpu.VMEM((width, columns), bf16),
            pltpu.VMEM((width, rows), bf16),
            pltpu.VMEM((width, columns), bf16),
            pltpu.VMEM((width, columns), bf16),
            pltpu.VMEM((width, columns), bf16),
            pltpu.VMEM((width, columns), bf16),
            pltpu.VMEM((probes, columns), bf16),
            pltpu.VMEM((probes, rows), bf16),
            pltpu.VMEM((2, fronts, *part), bf16),
            pltpu.VMEM((leaves, *child_map.shape[1:]), jnp.int32),
            pltpu.VMEM((3, 8, 128), jnp.int32),
            pltpu.VMEM((8, 128), jnp.int32),
            pltpu.SMEM((2, 8, 128), jnp.int32),
            pltpu.VMEM((5, 2, fronts, *part), bf16),
            pltpu.VMEM((5, 2, fronts, *part), bf16),
            pltpu.VMEM((2, FAR, *part), bf16),
            pltpu.VMEM((4, 2, *part), bf16),
            pltpu.VMEM((4, 2, fronts, *part), bf16),
            pltpu.VMEM((2, 2, *part), f32),
            pltpu.VMEM((2, *part), f32),
            pltpu.VMEM((leaves, 2, *part), f32),
            pltpu.VMEM((2, *part), f32),
            pltpu.VMEM((probes, width), f32),
            pltpu.VMEM((probes, width), f32),
            pltpu.VMEM((probes, width), f32),
            dma((4,)),
            dma((3,)),
            dma((leaves,)),
            dma((3,)),
            dma((5, 2, 2)),
            dma((5, 2, 2)),
            dma((2, 2)),
            dma((2,)),
            dma((4, 2, 2)),
            dma((4, 2, 2)),
            dma((2,)),
            dma((2,)),
            dma((2, 2)),
            dma((leaves, 2)),
            dma((2, 2)),
            dma((2, 2)),
            dma((2,)),
            dma,
        ],
        compiler_params=pltpu.CompilerParams(
            collective_id=0, has_side_effects=True, vmem_limit_bytes=48 * 1024 * 1024
        ),
        name="solves",
    )(*operands)


def solution(mesh):
    return jax.shard_map(
        shards,
        mesh=mesh,
        in_specs=(
            P(),
            P("leaf", "front", None),
            P("leaf", "front", None),
            P("leaf", "front", None),
            P("leaf", "front", None),
            P("leaf", None, None),
        ),
        out_specs=(P("leaf", None, "front"), P("leaf", None, "front")),
        check_vma=False,
    )
```

```python
import functools

import jax
import jax.numpy as jnp
from jax import lax
from jax.experimental import pallas as pl
from jax.experimental.pallas import tpu as pltpu
from jax.sharding import PartitionSpec as P

BLOCK = 64
MOD = 32749
MESH = pl.DeviceIdType.MESH
NT = (((1,), (1,)), ((), ()))
OFFSETS = (
    (2, 2), (2, 1), (1, 2), (2, 3), (3, 2), (2, 0), (0, 2), (1, 1),
    (3, 3), (1, 3), (3, 1), (1, 0), (0, 1), (3, 0), (0, 3), (0, 0),
)


def packed(values):
    word = sum(v << (2 * i) for i, v in enumerate(values))
    return word - (1 << 32) if word >= 1 << 31 else word


OFFSET_Z = packed([z for z, _ in OFFSETS])
OFFSET_Y = packed([y for _, y in OFFSETS])
CHIPS = 16
FAR_CHIPS = 5
FAR = 2 * FAR_CHIPS
CROSS = 3
TO_FIRST = (4, 8)
TO_SECOND = 12


def mod_prime(x):
    q = (x.astype(jnp.float32) * (1.0 / MOD)).astype(jnp.int32)
    r = x - q * MOD
    r = jnp.where(r < 0, r + MOD, r)
    return jnp.where(r >= MOD, r - MOD, r)


def probe_signs(seeds, node_id, columns, start, shape):
    index = node_id * columns + start + lax.broadcasted_iota(jnp.int32, shape, 1)
    wrapped = index >= MOD
    lower = jnp.where(wrapped, index - MOD, index)
    upper = jnp.where(wrapped, 1, 0)
    hashed = mod_prime(lower * 30011 + upper * 7717 + seeds)
    hashed = mod_prime(hashed * hashed)
    hashed = mod_prime(hashed * 21143 + lower)
    hashed = mod_prime(hashed * hashed + upper)
    return (1 - 2 * ((hashed >> 3) & 1)).astype(jnp.float32)


def kernel(
    fronts,
    probes,
    columns,
    width,
    seeds_hbm,
    maps_hbm,
    leaf_inv_hbm,
    leaf_upd_hbm,
    inner_inv_hbm,
    inner_upd_hbm,
    leaf_out,
    inner_out,
    seeds_s,
    leaf_inv,
    leaf_upd,
    inner_inv,
    inner_upd,
    to_slot,
    to_root,
    slot_root,
    root_inv,
    signs,
    leaf_all,
    carried,
    all_maps,
    table_v,
    table_in,
    table_s,
    send_part,
    recv_part,
    recv_cross,
    own_chunk,
    recv_all,
    hop_send,
    hop_up,
    hop_root,
    hop_root_x,
    leaf_y,
    inner_y,
    leaf_v,
    load_sem,
    small_sem,
    map_send,
    map_recv,
    part_send,
    part_recv,
    cross_send,
    cross_recv,
    all_send,
    all_recv,
    hop_up_send,
    hop_up_recv,
    hop_root_send,
    hop_root_recv,
    hop_x_send,
    hop_x_recv,
    bulk_send,
    bulk_recv,
):
    x = lax.axis_index("leaf")
    m = lax.axis_index("front")
    m_z, m_y, m_c = m // 8, lax.rem(m // 2, 4), lax.rem(m, 2)
    leaves = 4
    f32, bf16 = jnp.float32, jnp.bfloat16
    is_slot = (x == 0) | (x == 2)
    is_root = x == 1
    part_rows = probes // 2
    halves = (0, 1)

    def rows_of(h):
        return pl.ds(h * part_rows, part_rows)

    seed_copy = pltpu.make_async_copy(seeds_hbm, seeds_s, small_sem.at[0])
    map_copy = pltpu.make_async_copy(maps_hbm.at[0], all_maps.at[x], small_sem.at[1])
    seed_copy.start()
    map_copy.start()
    loads = [
        pltpu.make_async_copy(src.at[0], dst, load_sem.at[i])
        for i, (src, dst) in enumerate(
            (
                (leaf_inv_hbm, leaf_inv),
                (leaf_upd_hbm, leaf_upd),
                (inner_upd_hbm, inner_upd),
                (inner_inv_hbm, inner_inv),
            )
        )
    ]
    loads[0].start()
    loads[1].start()

    def peer(i):
        at = i & 30
        z = (m_z + (jnp.int32(OFFSET_Z) >> at)) & 3
        y = (m_y + (jnp.int32(OFFSET_Y) >> at)) & 3
        return z * 8 + y * 2 + ((m_c + 1 + i) & 1)

    barrier = pltpu.get_barrier_semaphore()

    def greet_front(i, carry):
        pl.semaphore_signal(barrier, inc=1, device_id=(x, peer(i)), device_id_type=MESH)
        return carry

    lax.fori_loop(0, fronts - 1, greet_front, 0)
    for i in range(1, leaves):
        pl.semaphore_signal(
            barrier, inc=1, device_id=(lax.rem(x + i, leaves), m), device_id_type=MESH
        )

    def map_to(to, kind):
        return pltpu.make_async_remote_copy(
            src_ref=maps_hbm.at[0],
            dst_ref=all_maps.at[x],
            send_sem=map_send.at[to],
            recv_sem=map_recv.at[kind],
            device_id=(to, m),
            device_id_type=MESH,
        )

    def slot_map_copy(to):
        return pltpu.make_async_remote_copy(
            src_ref=maps_hbm.at[0],
            dst_ref=all_maps.at[x],
            send_sem=map_send.at[0],
            recv_sem=map_recv.at[0],
            device_id=(to, m),
            device_id_type=MESH,
        )

    pieces = 16
    bulk_rows = width // pieces

    def bulk_copy(piece, to):
        rows = pl.ds(piece * bulk_rows, bulk_rows)
        return pltpu.make_async_remote_copy(
            src_ref=inner_inv_hbm.at[0, rows],
            dst_ref=root_inv.at[rows],
            send_sem=bulk_send.at[to // 2],
            recv_sem=bulk_recv,
            device_id=(to, m),
            device_id_type=MESH,
        )

    greeted = fronts - 1 + leaves - 1

    seed_copy.wait()
    seeds = jnp.zeros((probes, 1), jnp.int32)
    row = lax.broadcasted_iota(jnp.int32, (probes, 1), 0)
    for p in range(probes):
        seeds = jnp.where(row == p, seeds_s[p], seeds)

    piece = 512

    def make_signs(i, carry):
        start = pl.multiple_of(i * piece, piece)
        z = probe_signs(seeds, x, columns, start, (probes, piece))
        signs[:, pl.ds(start, piece)] = z.astype(bf16)
        return carry

    lax.fori_loop(0, columns // piece, make_signs, 0)

    def rows_times(vector, matrix):
        return lax.dot_general(vector, matrix[...], NT, preferred_element_type=f32)

    loads[0].wait()
    leaf_y[...] = rows_times(signs[...], leaf_inv)
    yb_leaf = leaf_y[...].astype(bf16)
    loads[1].wait()
    loads[2].start()
    loads[3].start()
    blocks = columns // BLOCK
    count = all_maps.shape[2]
    target = lax.broadcasted_iota(jnp.int32, (blocks, count), 0)
    source = lax.broadcasted_iota(jnp.int32, (blocks, count), 1) + 1
    lane = lax.broadcasted_iota(jnp.int32, (blocks, 128), 1)
    sub = lax.broadcasted_iota(jnp.int32, (blocks, 128), 0)

    def find(values, wanted):
        return jnp.max(jnp.where(values == wanted, source, 0), axis=1, keepdims=True)

    def as_row(column):
        return jnp.sum(jnp.where(lane == sub, column, 0), axis=0, keepdims=True)

    def slot_map():
        pair = all_maps[pl.ds((x // 2) * 2, 1)][0]
        return jnp.where(x % 2 == 0, pair[0:1], pair[1:2])

    def table_out(which):
        copy = pltpu.make_async_copy(table_v.at[which], table_s.at[which], small_sem.at[2])
        copy.start()
        copy.wait()

    table_v[...] = jnp.zeros(table_v.shape, jnp.int32)

    def child_table_copy(to):
        return pltpu.make_async_remote_copy(
            src_ref=table_v.at[2],
            dst_ref=table_in,
            send_sem=map_send.at[1],
            recv_sem=map_recv.at[2],
            device_id=(to, m),
            device_id_type=MESH,
        )

    @pl.when(is_slot)
    def _():
        map_copy.wait()
        pair = all_maps[pl.ds(x, 1)][0]
        table_v[0, 0:1, :] = as_row(find(pair[0:1], target))
        table_v[2, 0:1, :] = as_row(find(pair[1:2], target))
        pl.semaphore_wait(barrier, greeted)
        child_table_copy(x + 1).start()
        slot_map_copy(x + 1).start()
        table_out(0)

    wide = 2048

    def leaf_products(i, carry):
        at = pl.ds(pl.multiple_of(i * wide, wide), wide)
        leaf_all[:, at] = jnp.dot(
            yb_leaf, leaf_upd[:, at], preferred_element_type=f32
        ).astype(bf16)
        return carry

    lax.fori_loop(0, leaf_upd.shape[1] // wide, leaf_products, 0)
    @pl.when(jnp.logical_not(is_slot))
    def _():
        map_copy.wait()
        pl.semaphore_wait(barrier, greeted)

    @pl.when(is_root)
    def _():
        for to in (0, 2, 3):
            map_to(to, 1).start()
        for q in range(TO_FIRST[0]):
            bulk_copy(q, 0).start()
        for q in range(TO_SECOND):
            bulk_copy(q, 2).start()

    def pick(read, table, at, rows, order, write, low=0, high=blocks // 2, unroll=4):
        left_half = lax.broadcasted_iota(jnp.int32, (rows, 128), 1) < BLOCK

        def half(entry, side):
            block = jnp.maximum(entry - 1, 0)
            odd = jnp.full((rows, 128), block & 1, jnp.int32)
            found = jnp.full((rows, 128), entry, jnp.int32)
            tile = read((block >> 1) * 128).astype(f32)
            turned = pltpu.roll(tile, BLOCK, 1)
            here = jnp.where(odd == side, tile, turned)
            return jnp.where(found > 0, here, 0.0)

        def body(i, carry):
            j = order(i)
            first = half(table_s[table, at, 2 * j], 0)
            second = half(table_s[table, at, 2 * j + 1], 1)
            write(i, jnp.where(left_half, first, second).astype(bf16))
            return carry

        lax.fori_loop(low, high, body, 0, unroll=unroll)

    def pick_matrix(matrix, table, at, out):
        def write(j, tile):
            out[:, pl.ds(pl.multiple_of(j * 128, 128), 128)] = tile

        pick(lambda start: matrix[:, pl.ds(start, 128)], table, at, width, lambda j: j, write)

    def half_of(value, h):
        return value[h * part_rows : (h + 1) * part_rows]

    def pick_products(table, at, out, *part):
        def write(i, tile):
            for h in halves:
                out[h, i] = half_of(tile, h)

        pick(lambda start: leaf_all[:, pl.ds(start, 128)], table, at, probes, peer, write, *part)

    def send_each(low, high, to, src, dst, send_sem, recv_sem):
        def send(i, carry):
            pltpu.make_async_remote_copy(
                src_ref=src(i),
                dst_ref=dst(i),
                send_sem=send_sem,
                recv_sem=recv_sem,
                device_id=(to, peer(i)),
                device_id_type=MESH,
            ).start()
            return carry

        lax.fori_loop(low, high, send, 0, unroll=2)

    def wait_for(buffer, count, sem):
        part = buffer.at[pl.ds(0, count)]
        pltpu.make_async_copy(part, part, sem).wait()

    NEAR = fronts - 1 - FAR

    def send_far(which, h, to=None):
        if to is None:
            send_each(
                0, FAR, x,
                lambda i: send_part.at[which, h, i],
                lambda i: recv_part.at[which, h, i],
                part_send.at[which, h, 0], part_recv.at[which, h, 0],
            )
        else:
            send_each(
                0, FAR, to,
                lambda i: send_part.at[which, h, i],
                lambda i: recv_cross.at[h, i],
                cross_send.at[0, h], cross_recv.at[h],
            )

    def send_near(which, h):
        send_each(
            FAR, fronts - 1, x,
            lambda i: send_part.at[which, h, i],
            lambda i: recv_part.at[which, h, i],
            part_send.at[which, h, 1], part_recv.at[which, h, 1],
        )
        recv_part[which, h, fronts - 1] = send_part[which, h, fronts - 1]

    def columns_to(t):
        dz, dy = OFFSETS[t]
        chip = ((m_z + dz) & 3) * 4 + ((m_y + dy) & 3)
        return pl.ds(pl.multiple_of(chip * 256, 256), 256)

    def columns_from(t):
        dz, dy = OFFSETS[t]
        chip = ((m_z - dz) & 3) * 4 + ((m_y - dy) & 3)
        return pl.ds(pl.multiple_of(chip * 256, 256), 256)

    def sum_start(which, h, vector, matrix, more=None):
        def chips(low, high):
            for t in range(low, high):
                partial = jnp.dot(vector, matrix[:, columns_to(t)], preferred_element_type=f32)
                for core in (0, 1):
                    i = 2 * t + (m_c if core else 1 - m_c)
                    chunk = partial[:, core * width : (core + 1) * width]
                    if more is not None:
                        chunk = chunk + more[h, i].astype(f32)
                    send_part[which, h, i] = chunk.astype(bf16)

        chips(0, FAR_CHIPS)
        send_far(which, h)
        chips(FAR_CHIPS, CHIPS)
        send_near(which, h)

    def add_up(ref, low, high):
        sums = []
        for q in range(low, min(low + 4, high)):
            total = ref[q].astype(f32)
            for j in range(q + 4, high, 4):
                total = total + ref[j].astype(f32)
            sums.append(total)
        return (sums[0] + sums[1]) + (sums[2] + sums[3])

    def near_sum(which, h):
        wait_for(recv_part.at[which, h], NEAR, part_recv.at[which, h, 1])
        return add_up(recv_part.at[which, h], FAR, fronts)

    def far_sum(which, h):
        wait_for(recv_part.at[which, h], FAR, part_recv.at[which, h, 0])
        return add_up(recv_part.at[which, h], 0, FAR)

    def sum_finish(which, h):
        return near_sum(which, h) + far_sum(which, h)

    def cross_sum(h):
        wait_for(recv_cross.at[h], FAR, cross_recv.at[h])
        return add_up(recv_cross.at[h], 0, FAR)

    own_at = fronts - 2 + m_c

    def share(which, h, chunk_ref, low, high, to, send_sem):
        send_each(
            low, high, to,
            lambda i: chunk_ref,
            lambda i: recv_all.at[which, h, (i & 30) + m_c],
            send_sem, all_recv.at[which, h, 0 if high == FAR else 1],
        )

    def share_far(which, h, chunk_ref):
        share(which, h, chunk_ref, 0, FAR, x, all_send.at[which, h, 0])

    def share_near(which, h, chunk_ref):
        share(which, h, chunk_ref, FAR, fronts - 1, x, all_send.at[which, h, 1])

    def share_cross(which, h, chunk_ref, to):
        share(which, h, chunk_ref, 0, FAR, to, cross_send.at[1, h])

    def share_all(which, h, chunk_ref):
        share_far(which, h, chunk_ref)
        share_near(which, h, chunk_ref)
        recv_all[which, h, own_at] = chunk_ref[...]

    def shared_times(which, h, matrix, waits=True):
        total = None
        for far, low, high in ((1, FAR_CHIPS, CHIPS), (0, 0, FAR_CHIPS)):
            if waits:
                wait_for(recv_all.at[which, h], NEAR if far else FAR, all_recv.at[which, h, far])
            for t in range(low, high):
                vector = jnp.concatenate(
                    [recv_all[which, h, 2 * t], recv_all[which, h, 2 * t + 1]], axis=1
                )
                term = rows_times(vector, matrix.at[:, columns_from(t)])
                total = term if total is None else total + term
        return total

    def hop(src, dst, send_sem, recv_sem, to):
        return pltpu.make_async_remote_copy(
            src_ref=src,
            dst_ref=dst,
            send_sem=send_sem,
            recv_sem=recv_sem,
            device_id=(to, m),
            device_id_type=MESH,
        )

    LEAF_SUM, ROOT_SUM, ROOT_BACK, SLOT_BACK, LAST_SUM = 0, 1, 2, 3, 4
    SLOT_RHS, ROOT_RHS, ROOT_X, SLOT_X = 0, 1, 2, 3

    def up_copy(h, to):
        return hop(hop_send.at[0, h], hop_up.at[h], hop_up_send.at[h], hop_up_recv.at[h], to)

    def root_copy(h, i, origin, to):
        return hop(
            hop_root.at[origin, h], hop_root.at[origin, h], hop_root_send.at[i, h], hop_root_recv.at[origin, h], to
        )

    def root_x_copy(h, to):
        return hop(hop_send.at[1, h], hop_root_x.at[h], hop_x_send.at[1, h], hop_x_recv.at[0, h], to)

    def slot_x_copy(h, to):
        return hop(
            own_chunk.at[SLOT_X, h], recv_all.at[SLOT_X, h, own_at], hop_x_send.at[0, h], hop_x_recv.at[1, h], to
        )

    @pl.when(jnp.logical_not(is_slot))
    def _():
        child_table_copy(x).wait_recv()
        arrived = pltpu.make_async_copy(table_in, table_s.at[0], small_sem.at[2])
        arrived.start()
        arrived.wait()

    pick_products(0, 0, send_part.at[LEAF_SUM], 0, FAR, 5)

    def leaf_far(h):
        @pl.when(x != CROSS)
        def _():
            send_far(LEAF_SUM, h)

        @pl.when(x == CROSS)
        def _():
            send_far(LEAF_SUM, h, x - 1)

    leaf_far(0)
    pick_products(0, 0, send_part.at[LEAF_SUM], FAR, fronts, 11)
    send_near(LEAF_SUM, 0)
    leaf_far(1)
    send_near(LEAF_SUM, 1)

    @pl.when(jnp.logical_not(is_root))
    def _():
        map_to(0, 1).wait_recv()

    @pl.when(jnp.logical_not(is_slot))
    def _():
        slot_map_copy(x).wait_recv()

    root_pair = all_maps[1]
    root_map = jnp.where(x // 2 == 0, root_pair[0:1], root_pair[1:2])
    inner = find(root_map, target)
    through = find(slot_map(), jnp.where(inner == 0, -1, inner + (blocks - 1)))
    table_v[1, 0:1, :] = as_row(through)
    table_v[1, 1:2, :] = as_row(inner)
    table_out(1)

    @pl.when(jnp.logical_not(is_slot))
    def _():
        for h in halves:
            hop_send[0, h] = near_sum(LEAF_SUM, h)

            @pl.when(x != CROSS)
            def _():
                hop_send[0, h] = hop_send[0, h] + far_sum(LEAF_SUM, h)

            up_copy(h, x - 1).start()

        @pl.when(is_root)
        def _():
            for q in range(*TO_FIRST):
                bulk_copy(q, 0).start()

        pick_products(1, 0, send_part.at[ROOT_SUM])
        for h in halves:
            send_far(ROOT_SUM, h)
            send_near(ROOT_SUM, h)
        loads[2].wait()
        loads[3].wait()
        pick_matrix(leaf_upd, 0, 0, to_slot)
        pick_matrix(leaf_upd, 1, 0, to_root)
        for h in halves:
            hop_root[x, h] = sum_finish(ROOT_SUM, h)
            for i, to in enumerate((0, 2)):
                root_copy(h, i, x, to).start()

        @pl.when(is_root)
        def _():
            for q in range(TO_FIRST[1], pieces):
                bulk_copy(q, 0).start()
            for q in range(TO_SECOND, pieces):
                bulk_copy(q, 2).start()

    @pl.when(is_slot)
    def _():
        pick_products(1, 0, carried)
        loads[2].wait()
        pick_matrix(inner_upd, 1, 1, slot_root)
        slot_signs = probe_signs(seeds, x + 1 + leaves, columns, m * width, (probes, width))
        root_signs = probe_signs(seeds, 2 + leaves, columns, m * width, (probes, width))
        loads[3].wait()
        for h in halves:
            own_sum = sum_finish(LEAF_SUM, h)
            up_copy(h, x).wait_recv()

            @pl.when(x == CROSS - 1)
            def _():
                hop_up[h] = hop_up[h] + cross_sum(h)

            own_chunk[SLOT_RHS, h] = (half_of(slot_signs, h) - (own_sum + hop_up[h])).astype(bf16)
            share_all(SLOT_RHS, h, own_chunk.at[SLOT_RHS, h])
        pick_matrix(leaf_upd, 0, 0, to_slot)
        for h in halves:
            y_slot = shared_times(SLOT_RHS, h, inner_inv)
            inner_y[rows_of(h)] = y_slot
            sum_start(ROOT_SUM, h, y_slot.astype(bf16), slot_root, carried)
        pick_matrix(leaf_upd, 1, 0, to_root)
        for h in halves:
            hop_root[x, h] = sum_finish(ROOT_SUM, h)
            root_copy(h, 0, x, 2 - x).start()
        for h in halves:
            for origin in (1, 3):
                root_copy(h, 0, origin, x).wait_recv()
            root_copy(h, 0, 2 - x, x).wait_recv()
            total = (hop_root[0, h] + hop_root[1, h]) + (hop_root[2, h] + hop_root[3, h])
            own_chunk[ROOT_RHS, h] = (half_of(root_signs, h) - total).astype(bf16)
            share_all(ROOT_RHS, h, own_chunk.at[ROOT_RHS, h])
        pltpu.make_async_copy(root_inv, root_inv, bulk_recv).wait()
        for h in halves:
            y_root = shared_times(ROOT_RHS, h, root_inv)
            sum_start(ROOT_BACK, h, y_root.astype(bf16), root_inv)
        for h in halves:
            result = sum_finish(ROOT_BACK, h)
            own_chunk[ROOT_X, h] = result.astype(bf16)
            share_all(ROOT_X, h, own_chunk.at[ROOT_X, h])
            hop_send[1, h] = result
            root_x_copy(h, x + 1).start()
        for h in halves:
            v = shared_times(ROOT_X, h, slot_root)
            s = (inner_y[rows_of(h)] - v).astype(bf16)
            sum_start(SLOT_BACK, h, s, inner_inv)
        for h in halves:
            leaf_v[rows_of(h)] = leaf_y[rows_of(h)] - shared_times(ROOT_X, h, to_root, False)
        for h in halves:
            result = sum_finish(SLOT_BACK, h)
            chunk = own_chunk.at[SLOT_X, h]
            chunk[...] = result.astype(bf16)
            slot_x_copy(h, x + 1).start()
            share_cross(SLOT_X, h, chunk, x + 1)
            share_all(SLOT_X, h, chunk)
            inner_out[0, rows_of(h)] = result

    @pl.when(jnp.logical_not(is_slot))
    def _():
        for h in halves:
            root_x_copy(h, x).wait_recv()
            own_chunk[ROOT_X, h] = hop_root_x[h].astype(bf16)
            share_all(ROOT_X, h, own_chunk.at[ROOT_X, h])
            inner_out[0, rows_of(h)] = jnp.where(is_root, hop_root_x[h], 0.0)
        for h in halves:
            leaf_v[rows_of(h)] = leaf_y[rows_of(h)] - shared_times(ROOT_X, h, to_root)
        for h in halves:
            slot_x_copy(h, x).wait_recv()
            share_near(SLOT_X, h, recv_all.at[SLOT_X, h, own_at])

    for h in halves:
        v = shared_times(SLOT_X, h, to_slot)
        s = (leaf_v[rows_of(h)] - v).astype(bf16)
        sum_start(LAST_SUM, h, s, leaf_inv)
    for h in halves:
        leaf_out[0, rows_of(h)] = sum_finish(LAST_SUM, h)

    def far_left(buffer, sem):
        wait_for(buffer, FAR, sem)

    def near_left(buffer, sem):
        wait_for(buffer, NEAR, sem)

    for h in halves:
        for which in (LEAF_SUM, ROOT_SUM, LAST_SUM):
            near_left(send_part.at[which, h], part_send.at[which, h, 1])
        for which in (ROOT_SUM, LAST_SUM):
            far_left(send_part.at[which, h], part_send.at[which, h, 0])
        far_left(recv_all.at[ROOT_X, h], all_send.at[ROOT_X, h, 0])
        for which in (ROOT_X, SLOT_X):
            near_left(recv_all.at[which, h], all_send.at[which, h, 1])

    @pl.when(is_slot)
    def _():
        slot_map_copy(x + 1).wait_send()
        child_table_copy(x + 1).wait_send()
        for h in halves:
            for which in (ROOT_BACK, SLOT_BACK):
                far_left(send_part.at[which, h], part_send.at[which, h, 0])
                near_left(send_part.at[which, h], part_send.at[which, h, 1])
            for which in (SLOT_RHS, ROOT_RHS):
                far_left(recv_all.at[which, h], all_send.at[which, h, 0])
                near_left(recv_all.at[which, h], all_send.at[which, h, 1])
            root_copy(h, 0, x, 2 - x).wait_send()
            root_x_copy(h, x + 1).wait_send()
            far_left(recv_all.at[SLOT_X, h], all_send.at[SLOT_X, h, 0])
            far_left(recv_all.at[SLOT_X, h], cross_send.at[1, h])
            slot_x_copy(h, x + 1).wait_send()

    @pl.when(jnp.logical_not(is_slot))
    def _():
        for h in halves:
            up_copy(h, x - 1).wait_send()
            for i, to in enumerate((0, 2)):
                root_copy(h, i, x, to).wait_send()

    @pl.when(x == CROSS)
    def _():
        for h in halves:
            far_left(send_part.at[LEAF_SUM, h], cross_send.at[0, h])

    @pl.when(x != CROSS)
    def _():
        for h in halves:
            far_left(send_part.at[LEAF_SUM, h], part_send.at[LEAF_SUM, h, 0])

    @pl.when(is_root)
    def _():
        for to in (0, 2, 3):
            map_to(to, 1).wait_send()
        for to in (0, 2):
            pltpu.make_async_copy(root_inv, root_inv, bulk_send.at[to // 2]).wait()


def shards(probe_seeds, leaf_inverse, leaf_update, internal_inverse, internal_update, child_map):
    fronts = lax.axis_size("front")
    leaves = lax.axis_size("leaf")
    probes = probe_seeds.shape[0]
    width, columns = leaf_inverse.shape[1:]
    rows = leaf_update.shape[2]
    f32, bf16 = jnp.float32, jnp.bfloat16
    dma = pltpu.SemaphoreType.DMA
    vmem = pl.BlockSpec(memory_space=pltpu.VMEM)
    hbm = pl.BlockSpec(memory_space=pltpu.HBM)
    out = jax.ShapeDtypeStruct((1, probes, width), f32)
    part = (probes // 2, width)
    operands = [
        pltpu.with_memory_space_constraint(array, pltpu.HBM)
        for array in (
            probe_seeds, child_map, leaf_inverse, leaf_update, internal_inverse, internal_update,
        )
    ]
    return pl.pallas_call(
        functools.partial(kernel, fronts, probes, columns, width),
        out_shape=(out, out),
        in_specs=[hbm] * 6,
        out_specs=(vmem, vmem),
        scratch_shapes=[
            pltpu.SMEM((probes,), jnp.int32),
            pltpu.VMEM((width, columns), bf16),
            pltpu.VMEM((width, rows), bf16),
            pltpu.VMEM((width, columns), bf16),
            pltpu.VMEM((width, rows), bf16),
            pltpu.VMEM((width, columns), bf16),
            pltpu.VMEM((width, columns), bf16),
            pltpu.VMEM((width, columns), bf16),
            pltpu.VMEM((width, columns), bf16),
            pltpu.VMEM((probes, columns), bf16),
            pltpu.VMEM((probes, rows), bf16),
            pltpu.VMEM((2, fronts, *part), bf16),
            pltpu.VMEM((leaves, *child_map.shape[1:]), jnp.int32),
            pltpu.VMEM((3, 8, 128), jnp.int32),
            pltpu.VMEM((8, 128), jnp.int32),
            pltpu.SMEM((2, 8, 128), jnp.int32),
            pltpu.VMEM((5, 2, fronts, *part), bf16),
            pltpu.VMEM((5, 2, fronts, *part), bf16),
            pltpu.VMEM((2, FAR, *part), bf16),
            pltpu.VMEM((4, 2, *part), bf16),
            pltpu.VMEM((4, 2, fronts, *part), bf16),
            pltpu.VMEM((2, 2, *part), f32),
            pltpu.VMEM((2, *part), f32),
            pltpu.VMEM((leaves, 2, *part), f32),
            pltpu.VMEM((2, *part), f32),
            pltpu.VMEM((probes, width), f32),
            pltpu.VMEM((probes, width), f32),
            pltpu.VMEM((probes, width), f32),
            dma((4,)),
            dma((3,)),
            dma((leaves,)),
            dma((3,)),
            dma((5, 2, 2)),
            dma((5, 2, 2)),
            dma((2, 2)),
            dma((2,)),
            dma((4, 2, 2)),
            dma((4, 2, 2)),
            dma((2,)),
            dma((2,)),
            dma((2, 2)),
            dma((leaves, 2)),
            dma((2, 2)),
            dma((2, 2)),
            dma((2,)),
            dma,
        ],
        compiler_params=pltpu.CompilerParams(
            collective_id=0, has_side_effects=True, vmem_limit_bytes=48 * 1024 * 1024
        ),
        name="solves",
    )(*operands)


def solution(mesh):
    return jax.shard_map(
        shards,
        mesh=mesh,
        in_specs=(
            P(),
            P("leaf", "front", None),
            P("leaf", "front", None),
            P("leaf", "front", None),
            P("leaf", "front", None),
            P("leaf", None, None),
        ),
        out_specs=(P("leaf", None, "front"), P("leaf", None, "front")),
        check_vma=False,
    )
```

```python
import functools

import jax
import jax.numpy as jnp
from jax import lax
from jax.experimental import pallas as pl
from jax.experimental.pallas import tpu as pltpu
from jax.sharding import PartitionSpec as P

BLOCK = 64
MOD = 32749
MESH = pl.DeviceIdType.MESH
NT = (((1,), (1,)), ((), ()))
OFFSETS = (
    (2, 2), (2, 1), (1, 2), (2, 3), (3, 2), (2, 0), (0, 2), (1, 1),
    (3, 3), (1, 3), (3, 1), (1, 0), (0, 1), (3, 0), (0, 3), (0, 0),
)


def packed(values):
    word = sum(v << (2 * i) for i, v in enumerate(values))
    return word - (1 << 32) if word >= 1 << 31 else word


OFFSET_Z = packed([z for z, _ in OFFSETS])
OFFSET_Y = packed([y for _, y in OFFSETS])
CHIPS = 16
FAR_CHIPS = 5
FAR = 2 * FAR_CHIPS
CROSS = 3
TO_FIRST = (4, 8)
TO_SECOND = 12


def mod_prime(x):
    q = (x.astype(jnp.float32) * (1.0 / MOD)).astype(jnp.int32)
    r = x - q * MOD
    r = jnp.where(r < 0, r + MOD, r)
    return jnp.where(r >= MOD, r - MOD, r)


def probe_signs(seeds, node_id, columns, start, shape):
    index = node_id * columns + start + lax.broadcasted_iota(jnp.int32, shape, 1)
    wrapped = index >= MOD
    lower = jnp.where(wrapped, index - MOD, index)
    upper = jnp.where(wrapped, 1, 0)
    hashed = mod_prime(lower * 30011 + upper * 7717 + seeds)
    hashed = mod_prime(hashed * hashed)
    hashed = mod_prime(hashed * 21143 + lower)
    hashed = mod_prime(hashed * hashed + upper)
    return (1 - 2 * ((hashed >> 3) & 1)).astype(jnp.float32)


def kernel(
    fronts,
    probes,
    columns,
    width,
    seeds_hbm,
    maps_hbm,
    leaf_inv_hbm,
    leaf_upd_hbm,
    inner_inv_hbm,
    inner_upd_hbm,
    leaf_out,
    inner_out,
    seeds_s,
    leaf_inv,
    leaf_upd,
    inner_inv,
    inner_upd,
    to_slot,
    to_root,
    slot_root,
    root_inv,
    signs,
    leaf_all,
    carried,
    all_maps,
    table_v,
    table_in,
    table_s,
    send_part,
    recv_part,
    recv_cross,
    own_chunk,
    recv_all,
    hop_send,
    hop_up,
    hop_root,
    hop_root_x,
    leaf_y,
    inner_y,
    leaf_v,
    load_sem,
    small_sem,
    map_send,
    map_recv,
    part_send,
    part_recv,
    cross_send,
    cross_recv,
    all_send,
    all_recv,
    hop_up_send,
    hop_up_recv,
    hop_root_send,
    hop_root_recv,
    hop_x_send,
    hop_x_recv,
    bulk_send,
    bulk_recv,
):
    x = lax.axis_index("leaf")
    m = lax.axis_index("front")
    m_z, m_y, m_c = m // 8, lax.rem(m // 2, 4), lax.rem(m, 2)
    leaves = 4
    f32, bf16 = jnp.float32, jnp.bfloat16
    is_slot = (x == 0) | (x == 2)
    is_root = x == 1
    part_rows = probes // 2
    halves = (0, 1)

    def rows_of(h):
        return pl.ds(h * part_rows, part_rows)

    seed_copy = pltpu.make_async_copy(seeds_hbm, seeds_s, small_sem.at[0])
    map_copy = pltpu.make_async_copy(maps_hbm.at[0], all_maps.at[x], small_sem.at[1])
    seed_copy.start()
    map_copy.start()
    loads = [
        pltpu.make_async_copy(src.at[0], dst, load_sem.at[i])
        for i, (src, dst) in enumerate(
            (
                (leaf_inv_hbm, leaf_inv),
                (leaf_upd_hbm, leaf_upd),
                (inner_upd_hbm, inner_upd),
                (inner_inv_hbm, inner_inv),
            )
        )
    ]
    loads[0].start()
    loads[1].start()

    def peer(i):
        at = i & 30
        z = (m_z + (jnp.int32(OFFSET_Z) >> at)) & 3
        y = (m_y + (jnp.int32(OFFSET_Y) >> at)) & 3
        return z * 8 + y * 2 + ((m_c + 1 + i) & 1)

    barrier = pltpu.get_barrier_semaphore()

    def greet_front(i, carry):
        pl.semaphore_signal(barrier, inc=1, device_id=(x, peer(i)), device_id_type=MESH)
        return carry

    lax.fori_loop(0, fronts - 1, greet_front, 0)
    for i in range(1, leaves):
        pl.semaphore_signal(
            barrier, inc=1, device_id=(lax.rem(x + i, leaves), m), device_id_type=MESH
        )

    def map_to(to, kind):
        return pltpu.make_async_remote_copy(
            src_ref=maps_hbm.at[0],
            dst_ref=all_maps.at[x],
            send_sem=map_send.at[to],
            recv_sem=map_recv.at[kind],
            device_id=(to, m),
            device_id_type=MESH,
        )

    def slot_map_copy(to):
        return pltpu.make_async_remote_copy(
            src_ref=maps_hbm.at[0],
            dst_ref=all_maps.at[x],
            send_sem=map_send.at[0],
            recv_sem=map_recv.at[0],
            device_id=(to, m),
            device_id_type=MESH,
        )

    pieces = 16
    bulk_rows = width // pieces

    def bulk_copy(piece, to):
        rows = pl.ds(piece * bulk_rows, bulk_rows)
        return pltpu.make_async_remote_copy(
            src_ref=inner_inv_hbm.at[0, rows],
            dst_ref=root_inv.at[rows],
            send_sem=bulk_send.at[to // 2],
            recv_sem=bulk_recv,
            device_id=(to, m),
            device_id_type=MESH,
        )

    greeted = fronts - 1 + leaves - 1

    seed_copy.wait()
    seeds = jnp.zeros((probes, 1), jnp.int32)
    row = lax.broadcasted_iota(jnp.int32, (probes, 1), 0)
    for p in range(probes):
        seeds = jnp.where(row == p, seeds_s[p], seeds)

    piece = 512

    def make_signs(i, carry):
        start = pl.multiple_of(i * piece, piece)
        z = probe_signs(seeds, x, columns, start, (probes, piece))
        signs[:, pl.ds(start, piece)] = z.astype(bf16)
        return carry

    lax.fori_loop(0, columns // piece, make_signs, 0)

    def rows_times(vector, matrix):
        return lax.dot_general(vector, matrix[...], NT, preferred_element_type=f32)

    loads[0].wait()
    leaf_y[...] = rows_times(signs[...], leaf_inv)
    yb_leaf = leaf_y[...].astype(bf16)
    loads[1].wait()
    loads[2].start()
    loads[3].start()
    blocks = columns // BLOCK
    count = all_maps.shape[2]
    target = lax.broadcasted_iota(jnp.int32, (blocks, count), 0)
    source = lax.broadcasted_iota(jnp.int32, (blocks, count), 1) + 1
    lane = lax.broadcasted_iota(jnp.int32, (blocks, 128), 1)
    sub = lax.broadcasted_iota(jnp.int32, (blocks, 128), 0)

    def find(values, wanted):
        return jnp.max(jnp.where(values == wanted, source, 0), axis=1, keepdims=True)

    def as_row(column):
        return jnp.sum(jnp.where(lane == sub, column, 0), axis=0, keepdims=True)

    def slot_map():
        pair = all_maps[pl.ds((x // 2) * 2, 1)][0]
        return jnp.where(x % 2 == 0, pair[0:1], pair[1:2])

    def table_out(which):
        copy = pltpu.make_async_copy(table_v.at[which], table_s.at[which], small_sem.at[2])
        copy.start()
        copy.wait()

    table_v[...] = jnp.zeros(table_v.shape, jnp.int32)

    def child_table_copy(to):
        return pltpu.make_async_remote_copy(
            src_ref=table_v.at[2],
            dst_ref=table_in,
            send_sem=map_send.at[1],
            recv_sem=map_recv.at[2],
            device_id=(to, m),
            device_id_type=MESH,
        )

    @pl.when(is_slot)
    def _():
        map_copy.wait()
        pair = all_maps[pl.ds(x, 1)][0]
        table_v[0, 0:1, :] = as_row(find(pair[0:1], target))
        table_v[2, 0:1, :] = as_row(find(pair[1:2], target))
        pl.semaphore_wait(barrier, greeted)
        child_table_copy(x + 1).start()
        slot_map_copy(x + 1).start()
        table_out(0)

    wide = 2048

    def leaf_products(i, carry):
        at = pl.ds(pl.multiple_of(i * wide, wide), wide)
        leaf_all[:, at] = jnp.dot(
            yb_leaf, leaf_upd[:, at], preferred_element_type=f32
        ).astype(bf16)
        return carry

    lax.fori_loop(0, leaf_upd.shape[1] // wide, leaf_products, 0, unroll=4)
    @pl.when(jnp.logical_not(is_slot))
    def _():
        map_copy.wait()
        pl.semaphore_wait(barrier, greeted)

    @pl.when(is_root)
    def _():
        for to in (0, 2, 3):
            map_to(to, 1).start()
        for q in range(TO_FIRST[0]):
            bulk_copy(q, 0).start()
        for q in range(TO_SECOND):
            bulk_copy(q, 2).start()

    def pick(read, table, at, rows, order, write, low=0, high=blocks // 2, unroll=4):
        left_half = lax.broadcasted_iota(jnp.int32, (rows, 128), 1) < BLOCK

        def half(entry, side):
            block = jnp.maximum(entry - 1, 0)
            odd = jnp.full((rows, 128), block & 1, jnp.int32)
            found = jnp.full((rows, 128), entry, jnp.int32)
            tile = read((block >> 1) * 128).astype(f32)
            turned = pltpu.roll(tile, BLOCK, 1)
            here = jnp.where(odd == side, tile, turned)
            return jnp.where(found > 0, here, 0.0)

        def body(i, carry):
            j = order(i)
            first = half(table_s[table, at, 2 * j], 0)
            second = half(table_s[table, at, 2 * j + 1], 1)
            write(i, jnp.where(left_half, first, second).astype(bf16))
            return carry

        lax.fori_loop(low, high, body, 0, unroll=unroll)

    def pick_matrix(matrix, table, at, out):
        def write(j, tile):
            out[:, pl.ds(pl.multiple_of(j * 128, 128), 128)] = tile

        pick(lambda start: matrix[:, pl.ds(start, 128)], table, at, width, lambda j: j, write)

    def half_of(value, h):
        return value[h * part_rows : (h + 1) * part_rows]

    def pick_products(table, at, out, *part):
        def write(i, tile):
            for h in halves:
                out[h, i] = half_of(tile, h)

        pick(lambda start: leaf_all[:, pl.ds(start, 128)], table, at, probes, peer, write, *part)

    def send_each(low, high, to, src, dst, send_sem, recv_sem):
        def send(i, carry):
            pltpu.make_async_remote_copy(
                src_ref=src(i),
                dst_ref=dst(i),
                send_sem=send_sem,
                recv_sem=recv_sem,
                device_id=(to, peer(i)),
                device_id_type=MESH,
            ).start()
            return carry

        lax.fori_loop(low, high, send, 0, unroll=2)

    def wait_for(buffer, count, sem):
        part = buffer.at[pl.ds(0, count)]
        pltpu.make_async_copy(part, part, sem).wait()

    NEAR = fronts - 1 - FAR

    def send_far(which, h, to=None):
        if to is None:
            send_each(
                0, FAR, x,
                lambda i: send_part.at[which, h, i],
                lambda i: recv_part.at[which, h, i],
                part_send.at[which, h, 0], part_recv.at[which, h, 0],
            )
        else:
            send_each(
                0, FAR, to,
                lambda i: send_part.at[which, h, i],
                lambda i: recv_cross.at[h, i],
                cross_send.at[0, h], cross_recv.at[h],
            )

    def send_near(which, h):
        send_each(
            FAR, fronts - 1, x,
            lambda i: send_part.at[which, h, i],
            lambda i: recv_part.at[which, h, i],
            part_send.at[which, h, 1], part_recv.at[which, h, 1],
        )
        recv_part[which, h, fronts - 1] = send_part[which, h, fronts - 1]

    def columns_to(t):
        dz, dy = OFFSETS[t]
        chip = ((m_z + dz) & 3) * 4 + ((m_y + dy) & 3)
        return pl.ds(pl.multiple_of(chip * 256, 256), 256)

    def columns_from(t):
        dz, dy = OFFSETS[t]
        chip = ((m_z - dz) & 3) * 4 + ((m_y - dy) & 3)
        return pl.ds(pl.multiple_of(chip * 256, 256), 256)

    def sum_start(which, h, vector, matrix, more=None):
        def chips(low, high):
            for t in range(low, high):
                partial = jnp.dot(vector, matrix[:, columns_to(t)], preferred_element_type=f32)
                for core in (0, 1):
                    i = 2 * t + (m_c if core else 1 - m_c)
                    chunk = partial[:, core * width : (core + 1) * width]
                    if more is not None:
                        chunk = chunk + more[h, i].astype(f32)
                    send_part[which, h, i] = chunk.astype(bf16)

        chips(0, FAR_CHIPS)
        send_far(which, h)
        chips(FAR_CHIPS, CHIPS)
        send_near(which, h)

    def add_up(ref, low, high):
        sums = []
        for q in range(low, min(low + 4, high)):
            total = ref[q].astype(f32)
            for j in range(q + 4, high, 4):
                total = total + ref[j].astype(f32)
            sums.append(total)
        return (sums[0] + sums[1]) + (sums[2] + sums[3])

    def near_sum(which, h):
        wait_for(recv_part.at[which, h], NEAR, part_recv.at[which, h, 1])
        return add_up(recv_part.at[which, h], FAR, fronts)

    def far_sum(which, h):
        wait_for(recv_part.at[which, h], FAR, part_recv.at[which, h, 0])
        return add_up(recv_part.at[which, h], 0, FAR)

    def sum_finish(which, h):
        return near_sum(which, h) + far_sum(which, h)

    def cross_sum(h):
        wait_for(recv_cross.at[h], FAR, cross_recv.at[h])
        return add_up(recv_cross.at[h], 0, FAR)

    own_at = fronts - 2 + m_c

    def share(which, h, chunk_ref, low, high, to, send_sem):
        send_each(
            low, high, to,
            lambda i: chunk_ref,
            lambda i: recv_all.at[which, h, (i & 30) + m_c],
            send_sem, all_recv.at[which, h, 0 if high == FAR else 1],
        )

    def share_far(which, h, chunk_ref):
        share(which, h, chunk_ref, 0, FAR, x, all_send.at[which, h, 0])

    def share_near(which, h, chunk_ref):
        share(which, h, chunk_ref, FAR, fronts - 1, x, all_send.at[which, h, 1])

    def share_cross(which, h, chunk_ref, to):
        share(which, h, chunk_ref, 0, FAR, to, cross_send.at[1, h])

    def share_all(which, h, chunk_ref):
        share_far(which, h, chunk_ref)
        share_near(which, h, chunk_ref)
        recv_all[which, h, own_at] = chunk_ref[...]

    def shared_times(which, h, matrix, waits=True):
        total = None
        for far, low, high in ((1, FAR_CHIPS, CHIPS), (0, 0, FAR_CHIPS)):
            if waits:
                wait_for(recv_all.at[which, h], NEAR if far else FAR, all_recv.at[which, h, far])
            for t in range(low, high):
                vector = jnp.concatenate(
                    [recv_all[which, h, 2 * t], recv_all[which, h, 2 * t + 1]], axis=1
                )
                term = rows_times(vector, matrix.at[:, columns_from(t)])
                total = term if total is None else total + term
        return total

    def hop(src, dst, send_sem, recv_sem, to):
        return pltpu.make_async_remote_copy(
            src_ref=src,
            dst_ref=dst,
            send_sem=send_sem,
            recv_sem=recv_sem,
            device_id=(to, m),
            device_id_type=MESH,
        )

    LEAF_SUM, ROOT_SUM, ROOT_BACK, SLOT_BACK, LAST_SUM = 0, 1, 2, 3, 4
    SLOT_RHS, ROOT_RHS, ROOT_X, SLOT_X = 0, 1, 2, 3

    def up_copy(h, to):
        return hop(hop_send.at[0, h], hop_up.at[h], hop_up_send.at[h], hop_up_recv.at[h], to)

    def root_copy(h, i, origin, to):
        return hop(
            hop_root.at[origin, h], hop_root.at[origin, h], hop_root_send.at[i, h], hop_root_recv.at[origin, h], to
        )

    def root_x_copy(h, to):
        return hop(hop_send.at[1, h], hop_root_x.at[h], hop_x_send.at[1, h], hop_x_recv.at[0, h], to)

    def slot_x_copy(h, to):
        return hop(
            own_chunk.at[SLOT_X, h], recv_all.at[SLOT_X, h, own_at], hop_x_send.at[0, h], hop_x_recv.at[1, h], to
        )

    @pl.when(jnp.logical_not(is_slot))
    def _():
        child_table_copy(x).wait_recv()
        arrived = pltpu.make_async_copy(table_in, table_s.at[0], small_sem.at[2])
        arrived.start()
        arrived.wait()

    pick_products(0, 0, send_part.at[LEAF_SUM], 0, FAR, 5)

    def leaf_far(h):
        @pl.when(x != CROSS)
        def _():
            send_far(LEAF_SUM, h)

        @pl.when(x == CROSS)
        def _():
            send_far(LEAF_SUM, h, x - 1)

    leaf_far(0)
    pick_products(0, 0, send_part.at[LEAF_SUM], FAR, fronts, 11)
    send_near(LEAF_SUM, 0)
    leaf_far(1)
    send_near(LEAF_SUM, 1)

    @pl.when(jnp.logical_not(is_root))
    def _():
        map_to(0, 1).wait_recv()

    @pl.when(jnp.logical_not(is_slot))
    def _():
        slot_map_copy(x).wait_recv()

    root_pair = all_maps[1]
    root_map = jnp.where(x // 2 == 0, root_pair[0:1], root_pair[1:2])
    inner = find(root_map, target)
    through = find(slot_map(), jnp.where(inner == 0, -1, inner + (blocks - 1)))
    table_v[1, 0:1, :] = as_row(through)
    table_v[1, 1:2, :] = as_row(inner)
    table_out(1)

    @pl.when(jnp.logical_not(is_slot))
    def _():
        for h in halves:
            hop_send[0, h] = near_sum(LEAF_SUM, h)

            @pl.when(x != CROSS)
            def _():
                hop_send[0, h] = hop_send[0, h] + far_sum(LEAF_SUM, h)

            up_copy(h, x - 1).start()

        @pl.when(is_root)
        def _():
            for q in range(*TO_FIRST):
                bulk_copy(q, 0).start()

        pick_products(1, 0, send_part.at[ROOT_SUM])
        for h in halves:
            send_far(ROOT_SUM, h)
            send_near(ROOT_SUM, h)
        loads[2].wait()
        loads[3].wait()
        pick_matrix(leaf_upd, 0, 0, to_slot)
        pick_matrix(leaf_upd, 1, 0, to_root)
        for h in halves:
            hop_root[x, h] = sum_finish(ROOT_SUM, h)
            for i, to in enumerate((0, 2)):
                root_copy(h, i, x, to).start()

        @pl.when(is_root)
        def _():
            for q in range(TO_FIRST[1], pieces):
                bulk_copy(q, 0).start()
            for q in range(TO_SECOND, pieces):
                bulk_copy(q, 2).start()

    @pl.when(is_slot)
    def _():
        pick_products(1, 0, carried)
        loads[2].wait()
        pick_matrix(inner_upd, 1, 1, slot_root)
        slot_signs = probe_signs(seeds, x + 1 + leaves, columns, m * width, (probes, width))
        root_signs = probe_signs(seeds, 2 + leaves, columns, m * width, (probes, width))
        loads[3].wait()
        for h in halves:
            own_sum = sum_finish(LEAF_SUM, h)
            up_copy(h, x).wait_recv()

            @pl.when(x == CROSS - 1)
            def _():
                hop_up[h] = hop_up[h] + cross_sum(h)

            own_chunk[SLOT_RHS, h] = (half_of(slot_signs, h) - (own_sum + hop_up[h])).astype(bf16)
            share_all(SLOT_RHS, h, own_chunk.at[SLOT_RHS, h])
        pick_matrix(leaf_upd, 0, 0, to_slot)
        for h in halves:
            y_slot = shared_times(SLOT_RHS, h, inner_inv)
            inner_y[rows_of(h)] = y_slot
            sum_start(ROOT_SUM, h, y_slot.astype(bf16), slot_root, carried)
        pick_matrix(leaf_upd, 1, 0, to_root)
        for h in halves:
            hop_root[x, h] = sum_finish(ROOT_SUM, h)
            root_copy(h, 0, x, 2 - x).start()
        for h in halves:
            for origin in (1, 3):
                root_copy(h, 0, origin, x).wait_recv()
            root_copy(h, 0, 2 - x, x).wait_recv()
            total = (hop_root[0, h] + hop_root[1, h]) + (hop_root[2, h] + hop_root[3, h])
            own_chunk[ROOT_RHS, h] = (half_of(root_signs, h) - total).astype(bf16)
            share_all(ROOT_RHS, h, own_chunk.at[ROOT_RHS, h])
        pltpu.make_async_copy(root_inv, root_inv, bulk_recv).wait()
        for h in halves:
            y_root = shared_times(ROOT_RHS, h, root_inv)
            sum_start(ROOT_BACK, h, y_root.astype(bf16), root_inv)
        for h in halves:
            result = sum_finish(ROOT_BACK, h)
            own_chunk[ROOT_X, h] = result.astype(bf16)
            share_all(ROOT_X, h, own_chunk.at[ROOT_X, h])
            hop_send[1, h] = result
            root_x_copy(h, x + 1).start()
        for h in halves:
            v = shared_times(ROOT_X, h, slot_root)
            s = (inner_y[rows_of(h)] - v).astype(bf16)
            sum_start(SLOT_BACK, h, s, inner_inv)
        for h in halves:
            leaf_v[rows_of(h)] = leaf_y[rows_of(h)] - shared_times(ROOT_X, h, to_root, False)
        for h in halves:
            result = sum_finish(SLOT_BACK, h)
            chunk = own_chunk.at[SLOT_X, h]
            chunk[...] = result.astype(bf16)
            slot_x_copy(h, x + 1).start()
            share_cross(SLOT_X, h, chunk, x + 1)
            share_all(SLOT_X, h, chunk)
            inner_out[0, rows_of(h)] = result

    @pl.when(jnp.logical_not(is_slot))
    def _():
        for h in halves:
            root_x_copy(h, x).wait_recv()
            own_chunk[ROOT_X, h] = hop_root_x[h].astype(bf16)
            share_all(ROOT_X, h, own_chunk.at[ROOT_X, h])
            inner_out[0, rows_of(h)] = jnp.where(is_root, hop_root_x[h], 0.0)
        for h in halves:
            leaf_v[rows_of(h)] = leaf_y[rows_of(h)] - shared_times(ROOT_X, h, to_root)
        for h in halves:
            slot_x_copy(h, x).wait_recv()
            share_near(SLOT_X, h, recv_all.at[SLOT_X, h, own_at])

    for h in halves:
        v = shared_times(SLOT_X, h, to_slot)
        s = (leaf_v[rows_of(h)] - v).astype(bf16)
        sum_start(LAST_SUM, h, s, leaf_inv)
    for h in halves:
        leaf_out[0, rows_of(h)] = sum_finish(LAST_SUM, h)

    def far_left(buffer, sem):
        wait_for(buffer, FAR, sem)

    def near_left(buffer, sem):
        wait_for(buffer, NEAR, sem)

    for h in halves:
        for which in (LEAF_SUM, ROOT_SUM, LAST_SUM):
            near_left(send_part.at[which, h], part_send.at[which, h, 1])
        for which in (ROOT_SUM, LAST_SUM):
            far_left(send_part.at[which, h], part_send.at[which, h, 0])
        far_left(recv_all.at[ROOT_X, h], all_send.at[ROOT_X, h, 0])
        for which in (ROOT_X, SLOT_X):
            near_left(recv_all.at[which, h], all_send.at[which, h, 1])

    @pl.when(is_slot)
    def _():
        slot_map_copy(x + 1).wait_send()
        child_table_copy(x + 1).wait_send()
        for h in halves:
            for which in (ROOT_BACK, SLOT_BACK):
                far_left(send_part.at[which, h], part_send.at[which, h, 0])
                near_left(send_part.at[which, h], part_send.at[which, h, 1])
            for which in (SLOT_RHS, ROOT_RHS):
                far_left(recv_all.at[which, h], all_send.at[which, h, 0])
                near_left(recv_all.at[which, h], all_send.at[which, h, 1])
            root_copy(h, 0, x, 2 - x).wait_send()
            root_x_copy(h, x + 1).wait_send()
            far_left(recv_all.at[SLOT_X, h], all_send.at[SLOT_X, h, 0])
            far_left(recv_all.at[SLOT_X, h], cross_send.at[1, h])
            slot_x_copy(h, x + 1).wait_send()

    @pl.when(jnp.logical_not(is_slot))
    def _():
        for h in halves:
            up_copy(h, x - 1).wait_send()
            for i, to in enumerate((0, 2)):
                root_copy(h, i, x, to).wait_send()

    @pl.when(x == CROSS)
    def _():
        for h in halves:
            far_left(send_part.at[LEAF_SUM, h], cross_send.at[0, h])

    @pl.when(x != CROSS)
    def _():
        for h in halves:
            far_left(send_part.at[LEAF_SUM, h], part_send.at[LEAF_SUM, h, 0])

    @pl.when(is_root)
    def _():
        for to in (0, 2, 3):
            map_to(to, 1).wait_send()
        for to in (0, 2):
            pltpu.make_async_copy(root_inv, root_inv, bulk_send.at[to // 2]).wait()


def shards(probe_seeds, leaf_inverse, leaf_update, internal_inverse, internal_update, child_map):
    fronts = lax.axis_size("front")
    leaves = lax.axis_size("leaf")
    probes = probe_seeds.shape[0]
    width, columns = leaf_inverse.shape[1:]
    rows = leaf_update.shape[2]
    f32, bf16 = jnp.float32, jnp.bfloat16
    dma = pltpu.SemaphoreType.DMA
    vmem = pl.BlockSpec(memory_space=pltpu.VMEM)
    hbm = pl.BlockSpec(memory_space=pltpu.HBM)
    out = jax.ShapeDtypeStruct((1, probes, width), f32)
    part = (probes // 2, width)
    operands = [
        pltpu.with_memory_space_constraint(array, pltpu.HBM)
        for array in (
            probe_seeds, child_map, leaf_inverse, leaf_update, internal_inverse, internal_update,
        )
    ]
    return pl.pallas_call(
        functools.partial(kernel, fronts, probes, columns, width),
        out_shape=(out, out),
        in_specs=[hbm] * 6,
        out_specs=(vmem, vmem),
        scratch_shapes=[
            pltpu.SMEM((probes,), jnp.int32),
            pltpu.VMEM((width, columns), bf16),
            pltpu.VMEM((width, rows), bf16),
            pltpu.VMEM((width, columns), bf16),
            pltpu.VMEM((width, rows), bf16),
            pltpu.VMEM((width, columns), bf16),
            pltpu.VMEM((width, columns), bf16),
            pltpu.VMEM((width, columns), bf16),
            pltpu.VMEM((width, columns), bf16),
            pltpu.VMEM((probes, columns), bf16),
            pltpu.VMEM((probes, rows), bf16),
            pltpu.VMEM((2, fronts, *part), bf16),
            pltpu.VMEM((leaves, *child_map.shape[1:]), jnp.int32),
            pltpu.VMEM((3, 8, 128), jnp.int32),
            pltpu.VMEM((8, 128), jnp.int32),
            pltpu.SMEM((2, 8, 128), jnp.int32),
            pltpu.VMEM((5, 2, fronts, *part), bf16),
            pltpu.VMEM((5, 2, fronts, *part), bf16),
            pltpu.VMEM((2, FAR, *part), bf16),
            pltpu.VMEM((4, 2, *part), bf16),
            pltpu.VMEM((4, 2, fronts, *part), bf16),
            pltpu.VMEM((2, 2, *part), f32),
            pltpu.VMEM((2, *part), f32),
            pltpu.VMEM((leaves, 2, *part), f32),
            pltpu.VMEM((2, *part), f32),
            pltpu.VMEM((probes, width), f32),
            pltpu.VMEM((probes, width), f32),
            pltpu.VMEM((probes, width), f32),
            dma((4,)),
            dma((3,)),
            dma((leaves,)),
            dma((3,)),
            dma((5, 2, 2)),
            dma((5, 2, 2)),
            dma((2, 2)),
            dma((2,)),
            dma((4, 2, 2)),
            dma((4, 2, 2)),
            dma((2,)),
            dma((2,)),
            dma((2, 2)),
            dma((leaves, 2)),
            dma((2, 2)),
            dma((2, 2)),
            dma((2,)),
            dma,
        ],
        compiler_params=pltpu.CompilerParams(
            collective_id=0, has_side_effects=True, vmem_limit_bytes=48 * 1024 * 1024
        ),
        name="solves",
    )(*operands)


def solution(mesh):
    return jax.shard_map(
        shards,
        mesh=mesh,
        in_specs=(
            P(),
            P("leaf", "front", None),
            P("leaf", "front", None),
            P("leaf", "front", None),
            P("leaf", "front", None),
            P("leaf", None, None),
        ),
        out_specs=(P("leaf", None, "front"), P("leaf", None, "front")),
        check_vma=False,
    )
```
